32 devices in a mesh: tm: 8 (over z, x), space: 4 (over y, core).
Axes of the slice: x: 2, y: 2, z: 4, core: 2. Of those that a mesh axis runs over, the one named last changes fastest.
Arguments:
- forcing: float32 [8, 16, 32, 1024], P('tm', 'space'), may hold values from -6 to 6
- inv_density: bfloat16 [8, 16, 32, 1024], P('tm', 'space'), may hold values from 0.049804688 to 0.5
- wall_mask: int32 [16, 32, 1024], P('space'), may hold values 0 or 1
- guess: float32 [8, 16, 32, 1024], P('tm', 'space'), may hold values from -4 to 4
Outputs:
- pressure: float32 [8, 16, 32, 1024], P('tm', 'space')
- residual: float32 [8, 16, 32, 1024], P('tm', 'space')
The draws below stay inside these ranges and needn't reach their ends.
All inputs are finite; a program needn't handle non-finite values. No bound on the sum of `wall_mask` on one device may be relied on, other than what follows from the above.
Results may differ from the reference program's by a relative error of at most 0.0003.
Values sent between devices are 32-bit elements; how exact they have to be, the bound alone decides.
A program may use at most 64 MiB of HBM per device.

```python
import math
import jax
import jax.numpy as jnp

CELLS_X = 32
CELLS_Y = 1024
STEPS_DEV = 1
SWEEPS = 2
ITERS = 2
STEPS = 8
PLANES = 16
N_TM = 8


def set_ends(array, key, least, high):
    longest = array.shape.index(max(array.shape))
    spots = []
    for shift in (0, 1):
        where = [jax.random.randint(jax.random.fold_in(key, axis), (), 0, length) for axis, length in enumerate(array.shape)]
        where[longest] = (where[longest] + shift) % array.shape[longest]
        spots.append(tuple(where))
    return array.at[spots[0]].set(least).at[spots[1]].set(high)


def block_levels(rng, dims, split, least, top_value):
    loudness, own = 1.0, jax.random.fold_in(rng, 6)
    for axis_at, parts in split:
        heights = jnp.exp(jax.random.uniform(jax.random.fold_in(own, axis_at), (parts,), jnp.float32, least / len(split), top_value / len(split)))
        loudness = loudness * jnp.repeat(heights, dims[axis_at] // parts).reshape([-1 if axis == axis_at else 1 for axis in range(len(dims))])
    return loudness


def gaussian(stream_key, extent, deviation, bound, shards=(), dtype=jnp.bfloat16):
    drawn = deviation * jax.random.normal(stream_key, extent, jnp.float32)
    if shards:
        drawn = drawn * block_levels(stream_key, extent, shards, -0.22, 0.18)
    return jnp.clip(drawn, -bound, bound).astype(dtype)


def setup_inputs(seed: int = 0) -> dict:
    splits = jax.random.split(jax.random.key(seed), 5)
    forcing = gaussian(splits[0], (STEPS, PLANES, CELLS_X, CELLS_Y), 1.0, 6.0, ((0, 8), (1, 4)), jnp.float32)
    inv_density = jnp.clip(jnp.exp(math.log(0.5) - 2.306499 * jax.random.uniform(splits[1], (STEPS, PLANES, CELLS_X, CELLS_Y), jnp.float32) ** block_levels(splits[1], (STEPS, PLANES, CELLS_X, CELLS_Y), ((0, 8), (1, 4)), -0.2, 0.2)), 0.049804688, 0.5).astype(jnp.bfloat16)
    wall_mask = set_ends((jax.random.randint(splits[2], (PLANES, CELLS_X, CELLS_Y), 0, 8) < 7).astype(jnp.int32), jax.random.fold_in(splits[2], 1), 0, 1)
    guess = gaussian(splits[3], (STEPS, PLANES, CELLS_X, CELLS_Y), 0.3, 4.0, ((0, 8), (1, 4)), jnp.float32)
    return dict(forcing=forcing, inv_density=inv_density, wall_mask=wall_mask, guess=guess)


def neighbours(field):
    lead = [(0, 0)] * (field.ndim - 3)
    padded = jnp.pad(field, lead + [(1, 1), (1, 1), (1, 1)])
    beside = padded[..., 2:, 1:-1, 1:-1] + padded[..., :-2, 1:-1, 1:-1]
    beside = beside + padded[..., 1:-1, 2:, 1:-1] + padded[..., 1:-1, :-2, 1:-1]
    beside = beside + padded[..., 1:-1, 1:-1, 2:] + padded[..., 1:-1, 1:-1, :-2]
    return beside


def reference(forcing, inv_density, wall_mask, guess):
    shape = (N_TM, STEPS_DEV) + forcing.shape[1:]
    force_slab = forcing.reshape(shape)
    dens_slab = inv_density.astype(jnp.float32).reshape(shape)
    mask_float = wall_mask.astype(jnp.float32)
    pressure = guess
    for it in range(ITERS):
        old = pressure
        old_slab = old.reshape(shape)
        rolled_one = jnp.roll(old, 1, axis=0).reshape(shape)
        rolled_two = jnp.roll(old, 2, axis=0).reshape(shape)
        fresh = []
        for step in range(STEPS_DEV):
            if step >= 1:
                last_state = fresh[step - 1]
            else:
                last_state = rolled_one[:, step]
            if step >= 2:
                older_state = fresh[step - 2]
            else:
                older_state = rolled_two[:, step]
            source = force_slab[:, step] + 2.0 * last_state - 0.5 * older_state
            dens = dens_slab[:, step]
            value = old_slab[:, step]
            for sweep in range(SWEEPS):
                value = mask_float * ((source + dens * neighbours(value)) / (1.5 + 6.0 * dens))
            fresh.append(value)
        pressure = jnp.stack(fresh, axis=1).reshape(forcing.shape)
    dens_all = inv_density.astype(jnp.float32)
    last_all = jnp.roll(pressure, 1, axis=0)
    older_all = jnp.roll(pressure, 2, axis=0)
    residual = mask_float * (forcing - 1.5 * pressure + 2.0 * last_all - 0.5 * older_all
                             - dens_all * (6.0 * pressure - neighbours(pressure)))
    return pressure, residual
```

```python
import functools

import jax
import jax.numpy as jnp
from jax import lax
from jax.experimental import pallas as pl
from jax.experimental.pallas import tpu as pltpu
from jax.sharding import PartitionSpec as P

ITERS = 2
LANES = 128
PAD = 8
MESH = pl.DeviceIdType.MESH


def kernel(
    n_tm, n_space,
    f_hbm, k_hbm, m_hbm, g_hbm, p_out, r_out,
    V, ZB, XB, CB, F, K, M, W, KW, MD, MK, G,
    load_sem, zs, zr, xs, xr, hs, hr, h0, token_x, token_s,
):
    planes, height, width = F.shape
    chunks = width // LANES
    pairs = chunks // 2
    last = 2 * ITERS
    t = lax.axis_index("tm")
    s = lax.axis_index("space")
    even = lax.rem(t, 2) == 0
    odd = lax.rem(t, 2) == 1
    s_even = lax.rem(s, 2) == 0
    s_odd = lax.rem(s, 2) == 1
    partner = t + 1 - 2 * lax.rem(t, 2)
    ahead = lax.rem(t + 2, n_tm)
    behind = lax.rem(t + n_tm - 2, n_tm)
    has_lo = s > 0
    has_hi = s < n_space - 1
    inner = has_lo & has_hi
    rows = pl.ds(PAD, height)
    mine = pl.ds(1, planes)

    def lanes(c):
        return pl.ds(c * LANES, LANES)

    def scope(name):
        return jax.named_scope(name)

    load_g = [
        pltpu.make_async_copy(g_hbm.at[0, :, :, lanes(c)], V.at[0, c, mine, rows], load_sem.at[0])
        for c in range(chunks)
    ]
    loads = [
        pltpu.make_async_copy(k_hbm.at[0], K, load_sem.at[1]),
        pltpu.make_async_copy(m_hbm, M, load_sem.at[2]),
        pltpu.make_async_copy(f_hbm.at[0], F, load_sem.at[3]),
    ]

    barrier = pltpu.get_barrier_semaphore()
    pl.semaphore_signal(barrier, inc=1, device_id={"tm": behind}, device_id_type=MESH)

    @pl.when(even)
    def _():
        pl.semaphore_signal(barrier, inc=1, device_id={"tm": partner}, device_id_type=MESH)

    @pl.when(s_odd)
    def _():
        pl.semaphore_signal(barrier, inc=1, device_id={"space": s - 1}, device_id_type=MESH)

    @pl.when(s_odd & has_hi)
    def _():
        pl.semaphore_signal(barrier, inc=1, device_id={"space": s + 1}, device_id_type=MESH)

    for load in load_g + loads:
        load.start()

    with scope("bar"):
        for odd_t in (0, 1):
            for nb in (0, 1, 2):
                at_t = odd if odd_t else even
                at_s = (s_odd, s_even & jnp.logical_not(inner), s_even & inner)[nb]

                @pl.when(at_t & at_s)
                def _():
                    pl.semaphore_wait(barrier, 1 + odd_t + nb)

    def value(e, c):
        if e == 0:
            return g_hbm.at[0, :, :, lanes(c)]
        return V.at[2 * e, c, mine, rows]

    def plane(i, c, p):
        if i == 0:
            return g_hbm.at[0, p, :, lanes(c)]
        return V.at[i, c, 1 + p, rows]

    def z_copy(e, c, src):
        return pltpu.make_async_remote_copy(
            src, ZB.at[e, c], zs, zr.at[e, c], device_id={"tm": ahead}, device_id_type=MESH)

    def x_copy(e, c, src):
        return pltpu.make_async_remote_copy(
            src, XB.at[e, c], xs, xr.at[e, c], device_id={"tm": partner}, device_id_type=MESH)

    def halo_sem(i, c):
        return h0 if i == 0 else hr.at[lax.rem(i - 1, 2) if not isinstance(i, int) else (i - 1) % 2, c]

    def to_lo(i, c):
        return pltpu.make_async_remote_copy(
            plane(i, c, 0), V.at[i, c, planes + 1, rows], hs, halo_sem(i, c),
            device_id={"space": s - 1}, device_id_type=MESH)

    def to_hi(i, c):
        return pltpu.make_async_remote_copy(
            plane(i, c, planes - 1), V.at[i, c, 0, rows], hs, halo_sem(i, c),
            device_id={"space": s + 1}, device_id_type=MESH)

    def send_halo(i, c):
        @pl.when(has_lo)
        def _():
            to_lo(i, c).start()

        @pl.when(has_hi)
        def _():
            to_hi(i, c).start()

    def landed(ref, sem):
        pltpu.make_async_remote_copy(
            ref, ref, hs, sem, device_id={"tm": partner}, device_id_type=MESH).wait_recv()

    def left(ref, sem):
        pltpu.make_async_remote_copy(
            ref, ref, sem, h0, device_id={"tm": partner}, device_id_type=MESH).wait_send()

    def wait_halo(i, c):
        which = pl.ds(0, chunks) if i == 0 else pl.ds(c, 1)
        for nb, at in ((2, inner), (1, jnp.logical_not(inner))):
            @pl.when(at)
            def _(nb=nb):
                landed(V.at[i, which, pl.ds(0, nb), rows], halo_sem(i, c))

    with scope("send0"):
        @pl.when(even)
        def _():
            for c in (0, 2, 4):
                z_copy(0, c, value(0, c)).start()

        @pl.when(odd)
        def _():
            for c in (0, 2, 4, 1, 6, 3, 5, 7):
                z_copy(0, c, value(0, c)).start()
                if c in (0, 2, 4):
                    x_copy(0, c + 1, value(0, c + 1)).start()
            pl.semaphore_signal(token_x, inc=1, device_id={"tm": partner}, device_id_type=MESH)

        @pl.when(s_even & has_lo)
        def _():
            pl.semaphore_signal(token_s, inc=1, device_id={"space": s - 1}, device_id_type=MESH)

        @pl.when(s_even & has_hi)
        def _():
            pl.semaphore_signal(token_s, inc=1, device_id={"space": s + 1}, device_id_type=MESH)

    with scope("token_s"):
        @pl.when(s_odd & inner)
        def _():
            pl.semaphore_wait(token_s, 2)

        @pl.when(s_odd & jnp.logical_not(inner))
        def _():
            pl.semaphore_wait(token_s, 1)

    for c in range(chunks):
        send_halo(0, c)

    with scope("token_x"):
        @pl.when(even)
        def _():
            pl.semaphore_wait(token_x, 1)
            for c in range(chunks):
                x_copy(0, c, value(0, c)).start()

    edge = jnp.zeros((PAD, LANES), jnp.float32)
    flat = jnp.zeros((height, LANES), jnp.float32)

    def clear(n, _):
        i, c = n // chunks, lax.rem(n, chunks)
        for p in range(1, planes + 1):
            V[i, c, p, pl.ds(0, PAD), :] = edge
            V[i, c, p, pl.ds(PAD + height, PAD), :] = edge

        @pl.when(jnp.logical_not(has_lo))
        def _():
            V[i, c, 0, rows, :] = flat

        @pl.when(jnp.logical_not(has_hi))
        def _():
            V[i, c, planes + 1, rows, :] = flat
        return 0

    lax.fori_loop(0, (last + 1) * chunks, clear, 0)

    with scope("loads"):
        pltpu.make_async_copy(V.at[0, :, mine, rows], V.at[0, :, mine, rows], load_sem.at[0]).wait()
        for load in loads:
            load.wait()

    def prepare(c, _):
        at = pl.ds(pl.multiple_of(c * LANES, LANES), LANES)
        for p in range(planes):
            k = K[p, :, at].astype(jnp.float32)
            m = M[p, :, at].astype(jnp.float32)
            d = 1.5 + 6.0 * k
            w = m / d
            W[c, p] = w
            KW[c, p] = k * w
            MD[c, p] = m * d
            MK[c, p] = m * k
        return 0

    lax.fori_loop(0, chunks, prepare, 0)

    lane = lax.broadcasted_iota(jnp.int32, (height, LANES), 1)

    def over_planes(body):
        def step(p, _):
            body(p)
            return 0
        lax.fori_loop(0, planes, step, 0, unroll=True)

    def beside(i, c, p):
        mid = V[i, c, p + 1, rows, :]
        before = V[i, c - 1, p + 1, rows, :] if c > 0 else flat
        after = V[i, c + 1, p + 1, rows, :] if c < chunks - 1 else flat
        total = V[i, c, p, rows, :] + V[i, c, p + 2, rows, :]
        total = total + V[i, c, p + 1, pl.ds(PAD - 1, height), :]
        total = total + V[i, c, p + 1, pl.ds(PAD + 1, height), :]
        total = total + pltpu.roll(jnp.where(lane == LANES - 1, before, mid), 1, 1)
        total = total + pltpu.roll(jnp.where(lane == 0, after, mid), LANES - 1, 1)
        return mid, total

    def steps_before(e, c, p):
        z = ZB[e, c, p]
        both = 2.0 * XB[e, c, p] - 0.5 * z
        return both if c % 2 == 0 else jnp.where(even, z, both)

    def second(e, j):
        cz, cx = 2 * j, 2 * j + 1
        with scope(f"S{e}_{j}"):
            @pl.when(even)
            def _():
                landed(XB.at[e, cx], xr.at[e, cx])

                def mix(p):
                    CB[e, j, p] = 2.0 * XB[e, cx, p] - 0.5 * V[2 * e, cx, p + 1, rows, :]
                over_planes(mix)
                z_copy(e, cx, CB.at[e, j]).start()
                if e == 0 and j == 0:
                    z_copy(e, 6, value(e, 6)).start()

            @pl.when(odd)
            def _():
                landed(ZB.at[e, cz], zr.at[e, cz])
                x_copy(e, cz, ZB.at[e, cz]).start()
                if e == 0 and j == 1:
                    x_copy(e, 7, value(e, 7)).start()

    def ready(e, c):
        with scope(f"R{e}_{c}"):
            if c % 2 == 0:
                landed(XB.at[e, c], xr.at[e, c])

                @pl.when(even)
                def _():
                    landed(ZB.at[e, c], zr.at[e, c])
            else:
                landed(ZB.at[e, c], zr.at[e, c])

                @pl.when(odd)
                def _():
                    landed(XB.at[e, c], xr.at[e, c])

    def sweep_first(e, c):
        if e == 0:
            if c == 0:
                with scope("H0"):
                    wait_halo(0, 0)
        else:
            with scope(f"H{e}_{c}"):
                wait_halo(2 * e, c)

        with scope(f"A{e}_{c}"):
            def step(p):
                g = W[c, p] * (F[p, :, lanes(c)] + steps_before(e, c, p))
                G[c, p] = g
                V[2 * e + 1, c, p + 1, rows, :] = g + KW[c, p] * beside(2 * e, c, p)[1]
            over_planes(step)
        send_halo(2 * e + 1, c)

    def sweep_second(e, c):
        with scope(f"h{e}_{c}"):
            wait_halo(2 * e + 1, c)
        with scope(f"B{e}_{c}"):
            def step(p):
                v = G[c, p] + KW[c, p] * beside(2 * e + 1, c, p)[1]
                V[2 * e + 2, c, p + 1, rows, :] = v
                if e == ITERS - 1:
                    p_out[0, p, :, lanes(c)] = v
            over_planes(step)
        n = e + 1
        if c % 2 == 0:
            z_copy(n, c, value(n, c)).start()

            @pl.when(even)
            def _():
                x_copy(n, c, value(n, c)).start()
        else:
            x_copy(n, c, value(n, c)).start()

            @pl.when(odd)
            def _():
                z_copy(n, c, value(n, c)).start()
        send_halo(2 * n, c)

    def partial(c):
        with scope(f"Hl_{c}"):
            wait_halo(last, c)

        with scope(f"P_{c}"):
            def step(p):
                mid, total = beside(last, c, p)
                m = M[p, :, lanes(c)].astype(jnp.float32)
                G[c, p] = m * F[p, :, lanes(c)] - MD[c, p] * mid + MK[c, p] * total
            over_planes(step)

    def complete(c):
        with scope(f"C_{c}"):
            def step(p):
                m = M[p, :, lanes(c)].astype(jnp.float32)
                r_out[0, p, :, lanes(c)] = G[c, p] + m * steps_before(ITERS, c, p)
            over_planes(step)

    second(0, 0)
    for e in range(ITERS):
        second(e, 1)
        second(e, 2)
        for c in (0, 1):
            ready(e, c)
            sweep_first(e, c)
        second(e, 3)
        sweep_second(e, 0)
        for c in (2, 3):
            ready(e, c)
            sweep_first(e, c)
        sweep_second(e, 1)
        for c in (4, 5):
            ready(e, c)
            sweep_first(e, c)
        sweep_second(e, 2)
        sweep_second(e, 3)
        for c in (6, 7):
            ready(e, c)
            sweep_first(e, c)
        sweep_second(e, 4)
        second(e + 1, 0)
        sweep_second(e, 5)
        sweep_second(e, 6)
        sweep_second(e, 7)
    second(ITERS, 1)
    second(ITERS, 2)
    for c in (0, 1, 2, 3):
        partial(c)
    second(ITERS, 3)
    for c in (4, 5, 6, 7):
        partial(c)
    for c in range(chunks):
        ready(ITERS, c)
        complete(c)

    with scope("drain"):
        left(ZB, zs)
        left(XB, xs)
        for nb, at in ((2, inner), (1, jnp.logical_not(inner))):
            @pl.when(at)
            def _(nb=nb):
                left(V.at[:, :, pl.ds(0, nb), rows], hs)


def write_out(p_ref, r_ref, p_out, r_out, sem):
    planes = p_ref.shape[1]
    copies = []
    for i, (src, dst) in enumerate(((p_ref, p_out), (r_ref, r_out))):
        for p in range(planes):
            copies.append(pltpu.make_async_copy(src.at[0, p], dst.at[0, p], sem.at[i, p]))
    for copy in copies:
        copy.start()
    for copy in copies:
        copy.wait()


def solution(mesh):
    n_tm, n_space = mesh.shape["tm"], mesh.shape["space"]
    placed = (
        P("tm", "space", None, None),
        P("tm", "space", None, None),
        P("space", None, None),
        P("tm", "space", None, None),
    )

    def body(forcing, inv_density, wall_mask, guess):
        planes, height, width = wall_mask.shape
        chunks = width // LANES
        full = (planes, height, width)
        cut = (chunks, planes, height, LANES)
        exchanges = ITERS + 1
        values = 2 * ITERS + 1
        f32 = jnp.float32
        pressure, residual = pl.pallas_call(
            functools.partial(kernel, n_tm, n_space),
            out_shape=[pltpu.VMEM(guess.shape, f32)] * 2,
            in_specs=[pl.BlockSpec(memory_space=pl.ANY)] * 4,
            out_specs=[pl.BlockSpec(memory_space=pltpu.VMEM)] * 2,
            scratch_shapes=[
                pltpu.VMEM((values, chunks, planes + 2, height + 2 * PAD, LANES), f32),
                pltpu.VMEM((exchanges,) + cut, f32),
                pltpu.VMEM((exchanges,) + cut, f32),
                pltpu.VMEM((exchanges, chunks // 2) + cut[1:], f32),
                pltpu.VMEM(full, f32),
                pltpu.VMEM(full, inv_density.dtype),
                pltpu.VMEM(full, wall_mask.dtype),
                pltpu.VMEM(cut, f32),
                pltpu.VMEM(cut, f32),
                pltpu.VMEM(cut, f32),
                pltpu.VMEM(cut, f32),
                pltpu.VMEM(cut, f32),
                pltpu.SemaphoreType.DMA((4,)),
                pltpu.SemaphoreType.DMA,
                pltpu.SemaphoreType.DMA((exchanges, chunks)),
                pltpu.SemaphoreType.DMA,
                pltpu.SemaphoreType.DMA((exchanges, chunks)),
                pltpu.SemaphoreType.DMA,
                pltpu.SemaphoreType.DMA((2, chunks)),
                pltpu.SemaphoreType.DMA,
                pltpu.SemaphoreType.REGULAR,
                pltpu.SemaphoreType.REGULAR,
            ],
            compiler_params=pltpu.CompilerParams(collective_id=0, has_side_effects=True),
        )(forcing, inv_density, wall_mask, guess)
        return pl.pallas_call(
            write_out,
            out_shape=(jax.ShapeDtypeStruct(guess.shape, f32),) * 2,
            in_specs=[pl.BlockSpec(memory_space=pltpu.VMEM)] * 2,
            out_specs=(pl.BlockSpec(memory_space=pl.ANY),) * 2,
            scratch_shapes=[pltpu.SemaphoreType.DMA((2, planes))],
        )(*[pltpu.with_memory_space_constraint(v, pltpu.VMEM) for v in (pressure, residual)])

    return jax.shard_map(
        body,
        mesh=mesh,
        in_specs=placed,
        out_specs=(P("tm", "space", None, None), P("tm", "space", None, None)),
        check_vma=False,
    )
```

```python
import functools

import jax
import jax.numpy as jnp
from jax import lax
from jax.experimental import pallas as pl
from jax.experimental.pallas import tpu as pltpu
from jax.sharding import PartitionSpec as P

ITERS = 2
LANES = 128
PAD = 8
MESH = pl.DeviceIdType.MESH
FIRST_EVEN = (0, 2, 4)
FIRST_ODD = (0, 2, 4, 1, 6, 3, 5, 7)
FIRST_X = (1, 3, 5)
ORDER = "S00 E06 S01 X07 S02 R00 A00 R01 A01 B00 E10 O10 R02 A02 S03 R03 A03 B01 X11 O11 R04 A04 R05 A05 B02 E12 O12 B03 X13 R06 A06 S10 R07 A07 B04 E14 O14 B05 X15 B06 E16 O16 O13 B07 X17 O15 O17 S11 R10 A10 R11 A11 S12 B10 E20 O20 R12 A12 S13 R13 A13 B11 X21 R14 A14 R15 A15 B12 E22 O22 B13 X23 R16 A16 S20 R17 A17 B14 E24 O24 B15 X25 B16 E26 O26 O21 B17 X27 O23 O25 O27 S21 P0 P1 P2 P3 S22 P4 P5 P6 P7 S23 R20 C0 R21 C1 R22 C2 R23 C3 R24 C4 R25 C5 R26 C6 R27 C7"


def kernel(
    n_tm, n_space,
    f_hbm, k_hbm, m_hbm, g_hbm, p_out, r_out,
    V, ZB, XB, CB, F, K, M, W, KW, MD, MK, G,
    load_sem, zs, zr, xs, xr, hs, hr, h0, token_x, token_s,
):
    planes, height, width = F.shape
    chunks = width // LANES
    pairs = chunks // 2
    last = 2 * ITERS
    t = lax.axis_index("tm")
    s = lax.axis_index("space")
    even = lax.rem(t, 2) == 0
    odd = lax.rem(t, 2) == 1
    s_even = lax.rem(s, 2) == 0
    s_odd = lax.rem(s, 2) == 1
    partner = t + 1 - 2 * lax.rem(t, 2)
    ahead = lax.rem(t + 2, n_tm)
    behind = lax.rem(t + n_tm - 2, n_tm)
    has_lo = s > 0
    has_hi = s < n_space - 1
    inner = has_lo & has_hi
    rows = pl.ds(PAD, height)
    mine = pl.ds(1, planes)

    def lanes(c):
        return pl.ds(c * LANES, LANES)

    def scope(name):
        return jax.named_scope(name)

    load_g = [
        pltpu.make_async_copy(g_hbm.at[0, :, :, lanes(c)], V.at[0, c, mine, rows], load_sem.at[0])
        for c in range(chunks)
    ]
    loads = [
        pltpu.make_async_copy(k_hbm.at[0], K, load_sem.at[1]),
        pltpu.make_async_copy(m_hbm, M, load_sem.at[2]),
        pltpu.make_async_copy(f_hbm.at[0], F, load_sem.at[3]),
    ]

    barrier = pltpu.get_barrier_semaphore()
    pl.semaphore_signal(barrier, inc=1, device_id={"tm": behind}, device_id_type=MESH)

    @pl.when(even)
    def _():
        pl.semaphore_signal(barrier, inc=1, device_id={"tm": partner}, device_id_type=MESH)

    @pl.when(s_odd)
    def _():
        pl.semaphore_signal(barrier, inc=1, device_id={"space": s - 1}, device_id_type=MESH)

    @pl.when(s_odd & has_hi)
    def _():
        pl.semaphore_signal(barrier, inc=1, device_id={"space": s + 1}, device_id_type=MESH)

    for load in load_g + loads:
        load.start()

    with scope("bar"):
        for odd_t in (0, 1):
            for nb in (0, 1, 2):
                at_t = odd if odd_t else even
                at_s = (s_odd, s_even & jnp.logical_not(inner), s_even & inner)[nb]

                @pl.when(at_t & at_s)
                def _():
                    pl.semaphore_wait(barrier, 1 + odd_t + nb)

    def value(e, c):
        if e == 0:
            return g_hbm.at[0, :, :, lanes(c)]
        return V.at[2 * e, c, mine, rows]

    def plane(i, c, p):
        if i == 0:
            return g_hbm.at[0, p, :, lanes(c)]
        return V.at[i, c, 1 + p, rows]

    def z_copy(e, c, src):
        return pltpu.make_async_remote_copy(
            src, ZB.at[e, c], zs, zr.at[e, c], device_id={"tm": ahead}, device_id_type=MESH)

    def x_copy(e, c, src):
        return pltpu.make_async_remote_copy(
            src, XB.at[e, c], xs, xr.at[e, c], device_id={"tm": partner}, device_id_type=MESH)

    def halo_sem(i, c):
        return h0 if i == 0 else hr.at[lax.rem(i - 1, 2) if not isinstance(i, int) else (i - 1) % 2, c]

    def to_lo(i, c):
        return pltpu.make_async_remote_copy(
            plane(i, c, 0), V.at[i, c, planes + 1, rows], hs, halo_sem(i, c),
            device_id={"space": s - 1}, device_id_type=MESH)

    def to_hi(i, c):
        return pltpu.make_async_remote_copy(
            plane(i, c, planes - 1), V.at[i, c, 0, rows], hs, halo_sem(i, c),
            device_id={"space": s + 1}, device_id_type=MESH)

    def send_halo(i, c):
        @pl.when(has_lo)
        def _():
            to_lo(i, c).start()

        @pl.when(has_hi)
        def _():
            to_hi(i, c).start()

    def landed(ref, sem):
        pltpu.make_async_remote_copy(
            ref, ref, hs, sem, device_id={"tm": partner}, device_id_type=MESH).wait_recv()

    def left(ref, sem):
        pltpu.make_async_remote_copy(
            ref, ref, sem, h0, device_id={"tm": partner}, device_id_type=MESH).wait_send()

    def wait_halo(i, c):
        which = pl.ds(0, chunks) if i == 0 else pl.ds(c, 1)
        for nb, at in ((2, inner), (1, jnp.logical_not(inner))):
            @pl.when(at)
            def _(nb=nb):
                landed(V.at[i, which, pl.ds(0, nb), rows], halo_sem(i, c))

    with scope("send0"):
        @pl.when(even)
        def _():
            for c in FIRST_EVEN:
                z_copy(0, c, value(0, c)).start()

        @pl.when(odd)
        def _():
            for n, c in enumerate(FIRST_ODD):
                z_copy(0, c, value(0, c)).start()
                if n < len(FIRST_X):
                    x_copy(0, FIRST_X[n], value(0, FIRST_X[n])).start()
            pl.semaphore_signal(token_x, inc=1, device_id={"tm": partner}, device_id_type=MESH)

        @pl.when(s_even & has_lo)
        def _():
            pl.semaphore_signal(token_s, inc=1, device_id={"space": s - 1}, device_id_type=MESH)

        @pl.when(s_even & has_hi)
        def _():
            pl.semaphore_signal(token_s, inc=1, device_id={"space": s + 1}, device_id_type=MESH)

    with scope("token_s"):
        @pl.when(s_odd & inner)
        def _():
            pl.semaphore_wait(token_s, 2)

        @pl.when(s_odd & jnp.logical_not(inner))
        def _():
            pl.semaphore_wait(token_s, 1)

    for c in range(chunks):
        send_halo(0, c)

    with scope("token_x"):
        @pl.when(even)
        def _():
            pl.semaphore_wait(token_x, 1)
            for c in range(chunks):
                x_copy(0, c, value(0, c)).start()

    edge = jnp.zeros((PAD, LANES), jnp.float32)
    flat = jnp.zeros((height, LANES), jnp.float32)

    def clear(n, _):
        i, c = n // chunks, lax.rem(n, chunks)
        for p in range(1, planes + 1):
            V[i, c, p, pl.ds(0, PAD), :] = edge
            V[i, c, p, pl.ds(PAD + height, PAD), :] = edge

        @pl.when(jnp.logical_not(has_lo))
        def _():
            V[i, c, 0, rows, :] = flat

        @pl.when(jnp.logical_not(has_hi))
        def _():
            V[i, c, planes + 1, rows, :] = flat
        return 0

    lax.fori_loop(0, (last + 1) * chunks, clear, 0)

    with scope("loads"):
        pltpu.make_async_copy(V.at[0, :, mine, rows], V.at[0, :, mine, rows], load_sem.at[0]).wait()
        for load in loads:
            load.wait()

    def prepare(c, _):
        at = pl.ds(pl.multiple_of(c * LANES, LANES), LANES)
        for p in range(planes):
            k = K[p, :, at].astype(jnp.float32)
            m = M[p, :, at].astype(jnp.float32)
            d = 1.5 + 6.0 * k
            w = m / d
            W[c, p] = w
            KW[c, p] = k * w
            MD[c, p] = m * d
            MK[c, p] = m * k
        return 0

    lax.fori_loop(0, chunks, prepare, 0)

    lane = lax.broadcasted_iota(jnp.int32, (height, LANES), 1)

    def over_planes(body):
        def step(p, _):
            body(p)
            return 0
        lax.fori_loop(0, planes, step, 0, unroll=True)

    def beside(i, c, p):
        mid = V[i, c, p + 1, rows, :]
        before = V[i, c - 1, p + 1, rows, :] if c > 0 else flat
        after = V[i, c + 1, p + 1, rows, :] if c < chunks - 1 else flat
        total = V[i, c, p, rows, :] + V[i, c, p + 2, rows, :]
        total = total + V[i, c, p + 1, pl.ds(PAD - 1, height), :]
        total = total + V[i, c, p + 1, pl.ds(PAD + 1, height), :]
        total = total + pltpu.roll(jnp.where(lane == LANES - 1, before, mid), 1, 1)
        total = total + pltpu.roll(jnp.where(lane == 0, after, mid), LANES - 1, 1)
        return mid, total

    def steps_before(e, c, p):
        z = ZB[e, c, p]
        both = 2.0 * XB[e, c, p] - 0.5 * z
        return both if c % 2 == 0 else jnp.where(even, z, both)

    def second(e, j):
        cz, cx = 2 * j, 2 * j + 1
        with scope(f"S{e}_{j}"):
            @pl.when(even)
            def _():
                landed(XB.at[e, cx], xr.at[e, cx])

                def mix(p):
                    CB[e, j, p] = 2.0 * XB[e, cx, p] - 0.5 * V[2 * e, cx, p + 1, rows, :]
                over_planes(mix)
                z_copy(e, cx, CB.at[e, j]).start()

            @pl.when(odd)
            def _():
                landed(ZB.at[e, cz], zr.at[e, cz])
                x_copy(e, cz, ZB.at[e, cz]).start()

    def ready(e, c):
        with scope(f"R{e}_{c}"):
            if c % 2 == 0:
                landed(XB.at[e, c], xr.at[e, c])

                @pl.when(even)
                def _():
                    landed(ZB.at[e, c], zr.at[e, c])
            else:
                landed(ZB.at[e, c], zr.at[e, c])

                @pl.when(odd)
                def _():
                    landed(XB.at[e, c], xr.at[e, c])

    def sweep_first(e, c):
        if e == 0:
            if c == 0:
                with scope("H0"):
                    wait_halo(0, 0)
        else:
            with scope(f"H{e}_{c}"):
                wait_halo(2 * e, c)

        with scope(f"A{e}_{c}"):
            def step(p):
                g = W[c, p] * (F[p, :, lanes(c)] + steps_before(e, c, p))
                G[c, p] = g
                V[2 * e + 1, c, p + 1, rows, :] = g + KW[c, p] * beside(2 * e, c, p)[1]
            over_planes(step)
        send_halo(2 * e + 1, c)

    def sweep_second(e, c):
        with scope(f"h{e}_{c}"):
            wait_halo(2 * e + 1, c)
        with scope(f"B{e}_{c}"):
            def step(p):
                v = G[c, p] + KW[c, p] * beside(2 * e + 1, c, p)[1]
                V[2 * e + 2, c, p + 1, rows, :] = v
                if e == ITERS - 1:
                    p_out[0, p, :, lanes(c)] = v
            over_planes(step)
        n = e + 1

        @pl.when(even)
        def _():
            x_copy(n, c, value(n, c)).start()
        send_halo(2 * n, c)

    def even_z(e, c):
        @pl.when(even)
        def _():
            z_copy(e, c, value(e, c)).start()

    def odd_z(e, c):
        @pl.when(odd)
        def _():
            z_copy(e, c, value(e, c)).start()

    def own_x(e, c):
        @pl.when(odd)
        def _():
            x_copy(e, c, value(e, c)).start()

    def partial(c):
        with scope(f"Hl_{c}"):
            wait_halo(last, c)

        with scope(f"P_{c}"):
            def step(p):
                mid, total = beside(last, c, p)
                m = M[p, :, lanes(c)].astype(jnp.float32)
                G[c, p] = m * F[p, :, lanes(c)] - MD[c, p] * mid + MK[c, p] * total
            over_planes(step)

    def complete(c):
        with scope(f"C_{c}"):
            def step(p):
                m = M[p, :, lanes(c)].astype(jnp.float32)
                r_out[0, p, :, lanes(c)] = G[c, p] + m * steps_before(ITERS, c, p)
            over_planes(step)

    acts = {"S": second, "R": ready, "A": sweep_first, "B": sweep_second, "E": even_z, "O": odd_z, "P": partial, "C": complete, "X": own_x}
    for word in ORDER.split():
        acts[word[0]](*map(int, word[1:]))

    with scope("drain"):
        left(ZB, zs)
        left(XB, xs)
        for nb, at in ((2, inner), (1, jnp.logical_not(inner))):
            @pl.when(at)
            def _(nb=nb):
                left(V.at[:, :, pl.ds(0, nb), rows], hs)


def write_out(p_ref, r_ref, p_out, r_out, sem):
    planes = p_ref.shape[1]
    copies = []
    for i, (src, dst) in enumerate(((p_ref, p_out), (r_ref, r_out))):
        for p in range(planes):
            copies.append(pltpu.make_async_copy(src.at[0, p], dst.at[0, p], sem.at[i, p]))
    for copy in copies:
        copy.start()
    for copy in copies:
        copy.wait()


def solution(mesh):
    n_tm, n_space = mesh.shape["tm"], mesh.shape["space"]
    placed = (
        P("tm", "space", None, None),
        P("tm", "space", None, None),
        P("space", None, None),
        P("tm", "space", None, None),
    )

    def body(forcing, inv_density, wall_mask, guess):
        planes, height, width = wall_mask.shape
        chunks = width // LANES
        full = (planes, height, width)
        cut = (chunks, planes, height, LANES)
        exchanges = ITERS + 1
        values = 2 * ITERS + 1
        f32 = jnp.float32
        pressure, residual = pl.pallas_call(
            functools.partial(kernel, n_tm, n_space),
            out_shape=[pltpu.VMEM(guess.shape, f32)] * 2,
            in_specs=[pl.BlockSpec(memory_space=pl.ANY)] * 4,
            out_specs=[pl.BlockSpec(memory_space=pltpu.VMEM)] * 2,
            scratch_shapes=[
                pltpu.VMEM((values, chunks, planes + 2, height + 2 * PAD, LANES), f32),
                pltpu.VMEM((exchanges,) + cut, f32),
                pltpu.VMEM((exchanges,) + cut, f32),
                pltpu.VMEM((exchanges, chunks // 2) + cut[1:], f32),
                pltpu.VMEM(full, f32),
                pltpu.VMEM(full, inv_density.dtype),
                pltpu.VMEM(full, wall_mask.dtype),
                pltpu.VMEM(cut, f32),
                pltpu.VMEM(cut, f32),
                pltpu.VMEM(cut, f32),
                pltpu.VMEM(cut, f32),
                pltpu.VMEM(cut, f32),
                pltpu.SemaphoreType.DMA((4,)),
                pltpu.SemaphoreType.DMA,
                pltpu.SemaphoreType.DMA((exchanges, chunks)),
                pltpu.SemaphoreType.DMA,
                pltpu.SemaphoreType.DMA((exchanges, chunks)),
                pltpu.SemaphoreType.DMA,
                pltpu.SemaphoreType.DMA((2, chunks)),
                pltpu.SemaphoreType.DMA,
                pltpu.SemaphoreType.REGULAR,
                pltpu.SemaphoreType.REGULAR,
            ],
            compiler_params=pltpu.CompilerParams(collective_id=0, has_side_effects=True),
        )(forcing, inv_density, wall_mask, guess)
        return pl.pallas_call(
            write_out,
            out_shape=(jax.ShapeDtypeStruct(guess.shape, f32),) * 2,
            in_specs=[pl.BlockSpec(memory_space=pltpu.VMEM)] * 2,
            out_specs=(pl.BlockSpec(memory_space=pl.ANY),) * 2,
            scratch_shapes=[pltpu.SemaphoreType.DMA((2, planes))],
        )(*[pltpu.with_memory_space_constraint(v, pltpu.VMEM) for v in (pressure, residual)])

    return jax.shard_map(
        body,
        mesh=mesh,
        in_specs=placed,
        out_specs=(P("tm", "space", None, None), P("tm", "space", None, None)),
        check_vma=False,
    )
```

```python
import functools

import jax
import jax.numpy as jnp
from jax import lax
from jax.experimental import pallas as pl
from jax.experimental.pallas import tpu as pltpu
from jax.sharding import PartitionSpec as P

ITERS = 2
LANES = 128
PAD = 8
MESH = pl.DeviceIdType.MESH
FIRST_EVEN = (2, 0, 4)
FIRST_ODD = (0, 2, 1, 4, 6, 3, 5, 7)
FIRST_X = (1, 7, 3, 5)
WAY = ("ZXZXZXZX", "ZXZXZXZX", "ZXZXZXDX")
STEPS = (
    ("S", 0, 1), ("S", 0, 3), ("S", 0, 0), ("S", 0, 7), ("S", 0, 2), ("E", 0, 6), ("S", 0, 5), ("A", 0, 0),
    ("A", 0, 2), ("A", 0, 1), ("B", 0, 0), ("E", 1, 0), ("S", 0, 4), ("B", 0, 1), ("O", 1, 0), ("X", 1, 1),
    ("O", 1, 1), ("A", 0, 3), ("S", 0, 6), ("B", 0, 2), ("E", 1, 2), ("A", 0, 4), ("S", 1, 1), ("A", 0, 5),
    ("B", 0, 3), ("O", 1, 2), ("X", 1, 3), ("A", 0, 6), ("O", 1, 3), ("B", 0, 4), ("O", 1, 4), ("S", 1, 0),
    ("E", 1, 4), ("B", 0, 5), ("A", 0, 7), ("S", 1, 3), ("X", 1, 5), ("B", 0, 6), ("E", 1, 6), ("O", 1, 5),
    ("A", 1, 0), ("A", 1, 1), ("B", 0, 7), ("O", 1, 6), ("S", 1, 2), ("O", 1, 7), ("S", 1, 5), ("X", 1, 7),
    ("A", 1, 2), ("B", 1, 0), ("E", 2, 0), ("A", 1, 3), ("S", 1, 4), ("B", 1, 1), ("S", 1, 7), ("B", 1, 2),
    ("O", 2, 0), ("E", 2, 2), ("X", 2, 1), ("A", 1, 4), ("S", 2, 1), ("B", 1, 3), ("S", 1, 6), ("O", 2, 2),
    ("A", 1, 5), ("A", 1, 6), ("B", 1, 4), ("O", 2, 1), ("E", 2, 4), ("S", 2, 3), ("O", 2, 4), ("A", 1, 7),
    ("X", 2, 3), ("B", 1, 6), ("O", 2, 6), ("B", 1, 5), ("E", 2, 6), ("X", 2, 5), ("P", 2, 2), ("P", 2, 1),
    ("P", 2, 4), ("O", 2, 3), ("B", 1, 7), ("D", 2, 6), ("X", 2, 7), ("S", 2, 0), ("S", 2, 7), ("S", 2, 5),
    ("P", 2, 7), ("S", 2, 2), ("P", 2, 5), ("P", 2, 3), ("C", 2, 1), ("C", 2, 4), ("P", 2, 6), ("C", 2, 2),
    ("P", 2, 0), ("O", 2, 7), ("S", 2, 4), ("O", 2, 5), ("C", 2, 7), ("C", 2, 3), ("C", 2, 0), ("C", 2, 6),
    ("C", 2, 5),
)
FIRST_SWEPT = next(c for name, e, c in STEPS if name == "A")


def kernel(
    n_tm, n_space,
    f_hbm, k_hbm, m_hbm, g_hbm, p_out, r_out,
    V, ZB, XB, CB, F, K, M, W, KW, MD, MK, G,
    load_sem, zs, zr, xs, xr, hs, hr, h0, token_x, token_s, token_z, token_d,
):
    planes, height, width = F.shape
    chunks = width // LANES
    last = 2 * ITERS
    t = lax.axis_index("tm")
    s = lax.axis_index("space")
    even = lax.rem(t, 2) == 0
    odd = lax.rem(t, 2) == 1
    s_even = lax.rem(s, 2) == 0
    s_odd = lax.rem(s, 2) == 1
    partner = t + 1 - 2 * lax.rem(t, 2)
    ahead = lax.rem(t + 2, n_tm)
    behind = lax.rem(t + n_tm - 2, n_tm)
    next_up = lax.rem(t + 1, n_tm)
    prior = lax.rem(t + n_tm - 1, n_tm)
    has_lo = s > 0
    has_hi = s < n_space - 1
    inner = has_lo & has_hi
    rows = pl.ds(PAD, height)
    mine = pl.ds(1, planes)

    def lanes(c):
        return pl.ds(c * LANES, LANES)

    def scope(name):
        return jax.named_scope(name)

    load_g = [
        pltpu.make_async_copy(g_hbm.at[0, :, :, lanes(c)], V.at[0, c, mine, rows], load_sem.at[0])
        for c in range(chunks)
    ]
    loads = [
        pltpu.make_async_copy(k_hbm.at[0], K, load_sem.at[1]),
        pltpu.make_async_copy(m_hbm, M, load_sem.at[2]),
        pltpu.make_async_copy(f_hbm.at[0], F, load_sem.at[3]),
    ]

    barrier = pltpu.get_barrier_semaphore()
    first_z = t < 2
    last_z = t >= n_tm - 2
    near_z = (t >= n_tm - 4) & jnp.logical_not(last_z)
    by_token = t < n_tm - 4

    def greet(at, other):
        @pl.when(at)
        def _():
            pl.semaphore_signal(barrier, inc=1, device_id=other, device_id_type=MESH)

    def answer(at, token, other):
        @pl.when(at)
        def _():
            pl.semaphore_signal(token, inc=1, device_id=other, device_id_type=MESH)

    greet(first_z | last_z, {"tm": behind})
    greet(by_token, {"tm": ahead})
    greet(even, {"tm": partner})
    greet(s_odd, {"space": s - 1})
    greet(s_odd & has_hi, {"space": s + 1})

    for load in load_g + loads:
        load.start()

    one = jnp.int32(1)
    none = jnp.int32(0)
    told = jnp.where(first_z | last_z, none, one) + jnp.where(last_z | near_z, one, none) + jnp.where(odd, one, none)
    told = told + jnp.where(s_even & has_lo, one, none) + jnp.where(s_even & has_hi, one, none)
    with scope("bar"):
        for n in range(1, 6):
            @pl.when(told == n)
            def _(n=n):
                pl.semaphore_wait(barrier, n)
    answer(jnp.logical_not(first_z | last_z), token_z, {"tm": behind})
    answer(odd, token_x, {"tm": partner})
    answer(s_even & has_lo, token_s, {"space": s - 1})
    answer(s_even & has_hi, token_s, {"space": s + 1})

    def value(e, c):
        if e == 0:
            return g_hbm.at[0, :, :, lanes(c)]
        return V.at[2 * e, c, mine, rows]

    def plane(i, c, p):
        if i == 0:
            return g_hbm.at[0, p, :, lanes(c)]
        return V.at[i, c, 1 + p, rows]

    def z_copy(e, c, src):
        return pltpu.make_async_remote_copy(
            src, ZB.at[e, c], zs, zr.at[e, c], device_id={"tm": ahead}, device_id_type=MESH)

    def x_copy(e, c, src):
        return pltpu.make_async_remote_copy(
            src, XB.at[e, c], xs, xr.at[e, c], device_id={"tm": partner}, device_id_type=MESH)

    def halo_sem(i, c):
        return h0 if i == 0 else hr.at[(i - 1) % 2, c]

    def to_lo(i, c):
        return pltpu.make_async_remote_copy(
            plane(i, c, 0), V.at[i, c, planes + 1, rows], hs, halo_sem(i, c),
            device_id={"space": s - 1}, device_id_type=MESH)

    def to_hi(i, c):
        return pltpu.make_async_remote_copy(
            plane(i, c, planes - 1), V.at[i, c, 0, rows], hs, halo_sem(i, c),
            device_id={"space": s + 1}, device_id_type=MESH)

    def send_halo(i, c):
        @pl.when(has_lo)
        def _():
            to_lo(i, c).start()

        @pl.when(has_hi)
        def _():
            to_hi(i, c).start()

    def landed(ref, sem):
        pltpu.make_async_remote_copy(
            ref, ref, hs, sem, device_id={"tm": partner}, device_id_type=MESH).wait_recv()

    def left(ref, sem):
        pltpu.make_async_remote_copy(
            ref, ref, sem, h0, device_id={"tm": partner}, device_id_type=MESH).wait_send()

    def wait_halo(i, c):
        which = pl.ds(0, chunks) if i == 0 else pl.ds(c, 1)
        for nb, at in ((2, inner), (1, jnp.logical_not(inner))):
            @pl.when(at)
            def _(nb=nb):
                landed(V.at[i, which, pl.ds(0, nb), rows], halo_sem(i, c))

    def first_halos():
        for c in range(chunks):
            send_halo(0, c)

    with scope("send0"):
        @pl.when(odd)
        def _():
            for c in FIRST_X:
                x_copy(0, c, value(0, c)).start()

        @pl.when(s_even & jnp.logical_not(last_z))
        def _():
            first_halos()

        @pl.when(by_token)
        def _():
            pl.semaphore_wait(token_z, 1)

        @pl.when(even)
        def _():
            for c in FIRST_EVEN:
                z_copy(0, c, value(0, c)).start()

        @pl.when(odd)
        def _():
            for c in FIRST_ODD:
                z_copy(0, c, value(0, c)).start()

        @pl.when(s_even & last_z)
        def _():
            first_halos()

    with scope("token_x"):
        @pl.when(even)
        def _():
            pl.semaphore_wait(token_x, 1)
            for c in range(chunks):
                x_copy(0, c, value(0, c)).start()

    with scope("token_s"):
        @pl.when(s_odd & inner)
        def _():
            pl.semaphore_wait(token_s, 2)

        @pl.when(s_odd & jnp.logical_not(inner))
        def _():
            pl.semaphore_wait(token_s, 1)

        @pl.when(s_odd)
        def _():
            first_halos()

    edge = jnp.zeros((PAD, LANES), jnp.float32)
    flat = jnp.zeros((height, LANES), jnp.float32)

    def clear(c, _):
        for i in range(last + 1):
            for p in range(1, planes + 1):
                V[i, c, p, pl.ds(0, PAD), :] = edge
                V[i, c, p, pl.ds(PAD + height, PAD), :] = edge
        return 0

    def clear_plane(p):
        def body(c, _):
            for i in range(last + 1):
                V[i, c, p, rows, :] = flat
            return 0
        lax.fori_loop(0, chunks, body, 0)

    lax.fori_loop(0, chunks, clear, 0)

    @pl.when(jnp.logical_not(has_lo))
    def _():
        clear_plane(0)

    @pl.when(jnp.logical_not(has_hi))
    def _():
        clear_plane(planes + 1)

    with scope("loads"):
        pltpu.make_async_copy(V.at[0, :, mine, rows], V.at[0, :, mine, rows], load_sem.at[0]).wait()
        for load in loads:
            load.wait()

    def prepare(c, _):
        at = pl.ds(pl.multiple_of(c * LANES, LANES), LANES)
        for p in range(planes):
            k = K[p, :, at].astype(jnp.float32)
            m = M[p, :, at].astype(jnp.float32)
            d = 1.5 + 6.0 * k
            w = m / d
            W[c, p] = w
            KW[c, p] = k * w
            MD[c, p] = m * d
            MK[c, p] = m * k
        return 0

    lax.fori_loop(0, chunks, prepare, 0)

    lane = lax.broadcasted_iota(jnp.int32, (height, LANES), 1)

    def over_planes(body):
        def step(p, _):
            body(p)
            return 0
        lax.fori_loop(0, planes, step, 0, unroll=True)

    def beside(i, c, p):
        mid = V[i, c, p + 1, rows, :]
        before = V[i, c - 1, p + 1, rows, :] if c > 0 else flat
        after = V[i, c + 1, p + 1, rows, :] if c < chunks - 1 else flat
        total = V[i, c, p, rows, :] + V[i, c, p + 2, rows, :]
        total = total + V[i, c, p + 1, pl.ds(PAD - 1, height), :]
        total = total + V[i, c, p + 1, pl.ds(PAD + 1, height), :]
        total = total + pltpu.roll(jnp.where(lane == LANES - 1, before, mid), 1, 1)
        total = total + pltpu.roll(jnp.where(lane == 0, after, mid), LANES - 1, 1)
        return mid, total

    def steps_before(e, c, p):
        z = ZB[e, c, p]
        both = 2.0 * XB[e, c, p] - 0.5 * z
        return jnp.where(even, z, both) if WAY[e][c] == "X" else both

    waited = set()

    def second(e, c):
        with scope(f"S{e}_{c}"):
            if WAY[e][c] == "X":
                @pl.when(even)
                def _():
                    landed(XB.at[e, c], xr.at[e, c])

                    def mix(p):
                        CB[e, c, p] = 2.0 * XB[e, c, p] - 0.5 * V[2 * e, c, p + 1, rows, :]
                    over_planes(mix)
                    z_copy(e, c, CB.at[e, c]).start()
            else:
                @pl.when(odd)
                def _():
                    if (e, c) not in waited:
                        landed(ZB.at[e, c], zr.at[e, c])
                    x_copy(e, c, ZB.at[e, c]).start()
                waited.add((e, c))

    def direct(e, c):
        with scope("direct"):
            @pl.when(odd)
            def _():
                if (e, c) == first_direct:
                    pl.semaphore_wait(token_d, 1)
                pltpu.make_async_remote_copy(
                    value(e, c), XB.at[e, c], xs, xr.at[e, c],
                    device_id={"tm": next_up}, device_id_type=MESH).start()

    def ready(e, c):
        with scope(f"R{e}_{c}"):
            if WAY[e][c] == "X":
                landed(ZB.at[e, c], zr.at[e, c])

                @pl.when(odd)
                def _():
                    landed(XB.at[e, c], xr.at[e, c])
            elif WAY[e][c] == "Z":
                landed(XB.at[e, c], xr.at[e, c])
                if (e, c) in waited:
                    @pl.when(even)
                    def _():
                        landed(ZB.at[e, c], zr.at[e, c])
                else:
                    landed(ZB.at[e, c], zr.at[e, c])
                    waited.add((e, c))
            else:
                landed(XB.at[e, c], xr.at[e, c])
                landed(ZB.at[e, c], zr.at[e, c])

    def sweep_first(e, c):
        ready(e, c)
        if e == 0:
            if c == FIRST_SWEPT:
                with scope("H0"):
                    wait_halo(0, 0)
        else:
            with scope(f"H{e}_{c}"):
                wait_halo(2 * e, c)

        with scope(f"A{e}_{c}"):
            def step(p):
                g = W[c, p] * (F[p, :, lanes(c)] + steps_before(e, c, p))
                G[c, p] = g
                V[2 * e + 1, c, p + 1, rows, :] = g + KW[c, p] * beside(2 * e, c, p)[1]
            over_planes(step)
        send_halo(2 * e + 1, c)

    def sweep_second(e, c):
        with scope(f"h{e}_{c}"):
            wait_halo(2 * e + 1, c)
        with scope(f"B{e}_{c}"):
            def step(p):
                v = G[c, p] + KW[c, p] * beside(2 * e + 1, c, p)[1]
                V[2 * e + 2, c, p + 1, rows, :] = v
                if e == ITERS - 1:
                    p_out[0, p, :, lanes(c)] = v
            over_planes(step)
        n = e + 1

        @pl.when(even)
        def _():
            x_copy(n, c, value(n, c)).start()
        send_halo(2 * n, c)

    def even_z(e, c):
        @pl.when(even)
        def _():
            z_copy(e, c, value(e, c)).start()

    def odd_z(e, c):
        @pl.when(odd)
        def _():
            z_copy(e, c, value(e, c)).start()

    def own_x(e, c):
        @pl.when(odd)
        def _():
            x_copy(e, c, value(e, c)).start()

    def partial(e, c):
        with scope(f"Hl_{c}"):
            wait_halo(last, c)

        with scope(f"P_{c}"):
            def step(p):
                mid, total = beside(last, c, p)
                m = M[p, :, lanes(c)].astype(jnp.float32)
                G[c, p] = m * F[p, :, lanes(c)] - MD[c, p] * mid + MK[c, p] * total
            over_planes(step)

    def complete(e, c):
        ready(e, c)
        with scope(f"C_{c}"):
            def step(p):
                m = M[p, :, lanes(c)].astype(jnp.float32)
                r_out[0, p, :, lanes(c)] = G[c, p] + m * steps_before(ITERS, c, p)
            over_planes(step)

    acts = dict(S=second, A=sweep_first, B=sweep_second, E=even_z, O=odd_z, X=own_x, D=direct, P=partial, C=complete)
    relayed = next(c for name, e, c in STEPS if name == "A" and WAY[0][c] == "Z")
    first_direct = next(((e, c) for name, e, c in STEPS if name == "D"), None)
    for name, e, c in STEPS:
        acts[name](e, c)
        if first_direct and (name, e, c) == ("A", 0, relayed):
            answer(even, token_d, {"tm": prior})

    with scope("drain"):
        left(ZB, zs)
        left(XB, xs)
        for nb, at in ((2, inner), (1, jnp.logical_not(inner))):
            @pl.when(at)
            def _(nb=nb):
                left(V.at[:, :, pl.ds(0, nb), rows], hs)


def write_out(p_ref, r_ref, p_out, r_out, sem):
    copies = [
        pltpu.make_async_copy(src, dst, sem.at[i])
        for i, (src, dst) in enumerate(((p_ref, p_out), (r_ref, r_out)))
    ]
    for copy in copies:
        copy.start()
    for copy in copies:
        copy.wait()


def solution(mesh):
    n_tm, n_space = mesh.shape["tm"], mesh.shape["space"]
    placed = (
        P("tm", "space", None, None),
        P("tm", "space", None, None),
        P("space", None, None),
        P("tm", "space", None, None),
    )

    def body(forcing, inv_density, wall_mask, guess):
        planes, height, width = wall_mask.shape
        chunks = width // LANES
        full = (planes, height, width)
        cut = (chunks, planes, height, LANES)
        exchanges = ITERS + 1
        values = 2 * ITERS + 1
        f32 = jnp.float32
        pressure, residual = pl.pallas_call(
            functools.partial(kernel, n_tm, n_space),
            out_shape=[pltpu.VMEM(guess.shape, f32)] * 2,
            in_specs=[pl.BlockSpec(memory_space=pl.ANY)] * 4,
            out_specs=[pl.BlockSpec(memory_space=pltpu.VMEM)] * 2,
            scratch_shapes=[
                pltpu.VMEM((values, chunks, planes + 2, height + 2 * PAD, LANES), f32),
                pltpu.VMEM((exchanges,) + cut, f32),
                pltpu.VMEM((exchanges,) + cut, f32),
                pltpu.VMEM((exchanges,) + cut, f32),
                pltpu.VMEM(full, f32),
                pltpu.VMEM(full, inv_density.dtype),
                pltpu.VMEM(full, wall_mask.dtype),
                pltpu.VMEM(cut, f32),
                pltpu.VMEM(cut, f32),
                pltpu.VMEM(cut, f32),
                pltpu.VMEM(cut, f32),
                pltpu.VMEM(cut, f32),
                pltpu.SemaphoreType.DMA((4,)),
                pltpu.SemaphoreType.DMA,
                pltpu.SemaphoreType.DMA((exchanges, chunks)),
                pltpu.SemaphoreType.DMA,
                pltpu.SemaphoreType.DMA((exchanges, chunks)),
                pltpu.SemaphoreType.DMA,
                pltpu.SemaphoreType.DMA((2, chunks)),
                pltpu.SemaphoreType.DMA,
                pltpu.SemaphoreType.REGULAR,
                pltpu.SemaphoreType.REGULAR,
                pltpu.SemaphoreType.REGULAR,
                pltpu.SemaphoreType.REGULAR,
            ],
            compiler_params=pltpu.CompilerParams(collective_id=0, has_side_effects=True),
        )(forcing, inv_density, wall_mask, guess)
        return pl.pallas_call(
            write_out,
            out_shape=(jax.ShapeDtypeStruct(guess.shape, f32),) * 2,
            in_specs=[pl.BlockSpec(memory_space=pltpu.VMEM)] * 2,
            out_specs=(pl.BlockSpec(memory_space=pl.ANY),) * 2,
            scratch_shapes=[pltpu.SemaphoreType.DMA((2,))],
        )(*[pltpu.with_memory_space_constraint(v, pltpu.VMEM) for v in (pressure, residual)])

    return jax.shard_map(
        body,
        mesh=mesh,
        in_specs=placed,
        out_specs=(P("tm", "space", None, None), P("tm", "space", None, None)),
        check_vma=False,
    )
```

```python
import functools

import jax
import jax.numpy as jnp
from jax import lax
from jax.experimental import pallas as pl
from jax.experimental.pallas import tpu as pltpu
from jax.sharding import PartitionSpec as P

ITERS = 2
LANES = 128
PAD = 8
MESH = pl.DeviceIdType.MESH
FIRST_EVEN = (2, 4, 0)
FIRST_ODD = (0, 2, 1, 4, 3, 6, 5, 7)
FIRST_X = (1, 3, 5, 7)
WAY = ("ZXZXZXZX", "ZXZXZXZX", "ZZZXDXXZ")
STEPS = (
    ("S", 0, 1), ("S", 0, 3), ("S", 0, 5), ("S", 0, 0), ("S", 0, 7), ("E", 0, 6), ("S", 0, 2), ("A", 0, 1),
    ("A", 0, 0), ("A", 0, 2), ("B", 0, 0), ("E", 1, 0), ("S", 0, 4), ("O", 1, 0), ("B", 0, 1), ("X", 1, 1),
    ("A", 0, 3), ("B", 0, 2), ("O", 1, 1), ("E", 1, 2), ("A", 0, 4), ("S", 0, 6), ("A", 0, 5), ("S", 1, 1),
    ("B", 0, 3), ("X", 1, 3), ("B", 0, 4), ("E", 1, 4), ("O", 1, 2), ("A", 0, 6), ("A", 0, 7), ("B", 0, 5),
    ("X", 1, 5), ("O", 1, 3), ("S", 1, 3), ("B", 0, 6), ("E", 1, 6), ("S", 1, 5), ("O", 1, 4), ("O", 1, 6),
    ("B", 0, 7), ("S", 1, 0), ("A", 1, 1), ("X", 1, 7), ("A", 1, 0), ("S", 1, 2), ("O", 1, 5), ("S", 1, 7),
    ("O", 1, 7), ("B", 1, 0), ("A", 1, 2), ("E", 2, 0), ("A", 1, 3), ("B", 1, 1), ("E", 2, 1), ("O", 2, 1),
    ("S", 1, 4), ("S", 1, 6), ("A", 1, 4), ("B", 1, 2), ("E", 2, 2), ("O", 2, 0), ("B", 1, 3), ("X", 2, 3),
    ("A", 1, 6), ("A", 1, 5), ("S", 2, 3), ("O", 2, 2), ("A", 1, 7), ("B", 1, 6), ("X", 2, 6), ("B", 1, 4),
    ("B", 1, 5), ("D", 2, 4), ("X", 2, 5), ("E", 2, 4), ("B", 1, 7), ("O", 2, 7), ("E", 2, 7), ("S", 2, 1),
    ("S", 2, 0), ("O", 2, 6), ("O", 2, 3), ("S", 2, 6), ("S", 2, 2), ("S", 2, 5), ("O", 2, 4), ("S", 2, 7),
    ("O", 2, 5), ("P", 2, 0), ("P", 2, 1), ("P", 2, 2), ("P", 2, 3), ("P", 2, 4), ("P", 2, 5), ("P", 2, 6),
    ("P", 2, 7), ("C", 2, 2), ("C", 2, 1), ("C", 2, 0), ("C", 2, 3), ("C", 2, 4), ("C", 2, 7), ("C", 2, 6),
    ("C", 2, 5),
)
FIRST_SWEPT = next(c for name, e, c in STEPS if name == "A")


def kernel(
    n_tm, n_space,
    f_hbm, k_hbm, m_hbm, g_hbm, p_out, r_out,
    V, ZB, XB, CB, F, K, M, W, FW, KW, MD, MK, G,
    load_sem, zs, zr, xs, xr, hs, hr, h0, token_x, token_s, token_z, token_d,
):
    planes, height, width = F.shape
    chunks = width // LANES
    last = 2 * ITERS
    t = lax.axis_index("tm")
    s = lax.axis_index("space")
    even = lax.rem(t, 2) == 0
    odd = lax.rem(t, 2) == 1
    s_even = lax.rem(s, 2) == 0
    s_odd = lax.rem(s, 2) == 1
    partner = t + 1 - 2 * lax.rem(t, 2)
    ahead = lax.rem(t + 2, n_tm)
    behind = lax.rem(t + n_tm - 2, n_tm)
    next_up = lax.rem(t + 1, n_tm)
    prior = lax.rem(t + n_tm - 1, n_tm)
    has_lo = s > 0
    has_hi = s < n_space - 1
    inner = has_lo & has_hi
    rows = pl.ds(PAD, height)
    mine = pl.ds(1, planes)

    def lanes(c):
        return pl.ds(c * LANES, LANES)

    def scope(name):
        return jax.named_scope(name)

    load_g = [
        pltpu.make_async_copy(g_hbm.at[0, :, :, lanes(c)], V.at[0, c, mine, rows], load_sem.at[0])
        for c in range(chunks)
    ]
    loads = [
        pltpu.make_async_copy(k_hbm.at[0], K, load_sem.at[1]),
        pltpu.make_async_copy(m_hbm, M, load_sem.at[2]),
        pltpu.make_async_copy(f_hbm.at[0], F, load_sem.at[3]),
    ]

    barrier = pltpu.get_barrier_semaphore()
    first_z = t < 2
    last_z = t >= n_tm - 2
    near_z = (t >= n_tm - 4) & jnp.logical_not(last_z)
    by_token = t < n_tm - 4

    def greet(at, other):
        @pl.when(at)
        def _():
            pl.semaphore_signal(barrier, inc=1, device_id=other, device_id_type=MESH)

    def answer(at, token, other):
        @pl.when(at)
        def _():
            pl.semaphore_signal(token, inc=1, device_id=other, device_id_type=MESH)

    greet(first_z | last_z, {"tm": behind})
    greet(by_token, {"tm": ahead})
    greet(even, {"tm": partner})
    greet(s_odd, {"space": s - 1})
    greet(s_odd & has_hi, {"space": s + 1})

    for load in load_g + loads:
        load.start()

    one = jnp.int32(1)
    none = jnp.int32(0)
    told = jnp.where(first_z | last_z, none, one) + jnp.where(last_z | near_z, one, none) + jnp.where(odd, one, none)
    told = told + jnp.where(s_even & has_lo, one, none) + jnp.where(s_even & has_hi, one, none)
    with scope("bar"):
        for n in range(1, 6):
            @pl.when(told == n)
            def _(n=n):
                pl.semaphore_wait(barrier, n)
    answer(jnp.logical_not(first_z | last_z), token_z, {"tm": behind})
    answer(odd, token_x, {"tm": partner})
    answer(s_even & has_lo, token_s, {"space": s - 1})
    answer(s_even & has_hi, token_s, {"space": s + 1})

    def value(e, c):
        if e == 0:
            return g_hbm.at[0, :, :, lanes(c)]
        return V.at[2 * e, c, mine, rows]

    def plane(i, c, p):
        if i == 0:
            return g_hbm.at[0, p, :, lanes(c)]
        return V.at[i, c, 1 + p, rows]

    def z_copy(e, c, src):
        return pltpu.make_async_remote_copy(
            src, ZB.at[e, c], zs, zr.at[e, c], device_id={"tm": ahead}, device_id_type=MESH)

    def x_copy(e, c, src):
        return pltpu.make_async_remote_copy(
            src, XB.at[e, c], xs, xr.at[e, c], device_id={"tm": partner}, device_id_type=MESH)

    def halo_sem(i, c):
        return h0 if i == 0 else hr.at[(i - 1) % 2, c]

    def to_lo(i, c):
        return pltpu.make_async_remote_copy(
            plane(i, c, 0), V.at[i, c, planes + 1, rows], hs, halo_sem(i, c),
            device_id={"space": s - 1}, device_id_type=MESH)

    def to_hi(i, c):
        return pltpu.make_async_remote_copy(
            plane(i, c, planes - 1), V.at[i, c, 0, rows], hs, halo_sem(i, c),
            device_id={"space": s + 1}, device_id_type=MESH)

    def send_halo(i, c):
        @pl.when(has_lo)
        def _():
            to_lo(i, c).start()

        @pl.when(has_hi)
        def _():
            to_hi(i, c).start()

    def landed(ref, sem):
        pltpu.make_async_remote_copy(
            ref, ref, hs, sem, device_id={"tm": partner}, device_id_type=MESH).wait_recv()

    def left(ref, sem):
        pltpu.make_async_remote_copy(
            ref, ref, sem, h0, device_id={"tm": partner}, device_id_type=MESH).wait_send()

    def wait_halo(i, c):
        which = pl.ds(0, chunks) if i == 0 else pl.ds(c, 1)
        for nb, at in ((2, inner), (1, jnp.logical_not(inner))):
            @pl.when(at)
            def _(nb=nb):
                landed(V.at[i, which, pl.ds(0, nb), rows], halo_sem(i, c))

    def first_halos():
        for c in range(chunks):
            send_halo(0, c)

    with scope("send0"):
        @pl.when(odd)
        def _():
            for c in FIRST_X:
                x_copy(0, c, value(0, c)).start()

        @pl.when(s_even & jnp.logical_not(last_z))
        def _():
            first_halos()

        @pl.when(by_token)
        def _():
            pl.semaphore_wait(token_z, 1)

        @pl.when(even)
        def _():
            for c in FIRST_EVEN:
                z_copy(0, c, value(0, c)).start()

        @pl.when(odd)
        def _():
            for c in FIRST_ODD:
                z_copy(0, c, value(0, c)).start()

        @pl.when(s_even & last_z)
        def _():
            first_halos()

    with scope("token_x"):
        @pl.when(even)
        def _():
            pl.semaphore_wait(token_x, 1)
            for c in range(chunks):
                x_copy(0, c, value(0, c)).start()

    with scope("token_s"):
        @pl.when(s_odd & inner)
        def _():
            pl.semaphore_wait(token_s, 2)

        @pl.when(s_odd & jnp.logical_not(inner))
        def _():
            pl.semaphore_wait(token_s, 1)

        @pl.when(s_odd)
        def _():
            first_halos()

    edge = jnp.zeros((PAD, LANES), jnp.float32)
    flat = jnp.zeros((height, LANES), jnp.float32)

    def clear(c, _):
        for i in range(last + 1):
            for p in range(1, planes + 1):
                V[i, c, p, pl.ds(0, PAD), :] = edge
                V[i, c, p, pl.ds(PAD + height, PAD), :] = edge
        return 0

    def clear_plane(p):
        def body(c, _):
            for i in range(last + 1):
                V[i, c, p, rows, :] = flat
            return 0
        lax.fori_loop(0, chunks, body, 0)

    lax.fori_loop(0, chunks, clear, 0)

    @pl.when(jnp.logical_not(has_lo))
    def _():
        clear_plane(0)

    @pl.when(jnp.logical_not(has_hi))
    def _():
        clear_plane(planes + 1)

    with scope("loads"):
        pltpu.make_async_copy(V.at[0, :, mine, rows], V.at[0, :, mine, rows], load_sem.at[0]).wait()
        for load in loads:
            load.wait()

    def prepare(c, _):
        at = pl.ds(pl.multiple_of(c * LANES, LANES), LANES)
        for p in range(planes):
            k = K[p, :, at].astype(jnp.float32)
            m = M[p, :, at].astype(jnp.float32)
            d = 1.5 + 6.0 * k
            w = m / d
            W[c, p] = w
            FW[c, p] = w * F[p, :, at]
            KW[c, p] = k * w
            MD[c, p] = m * d
            MK[c, p] = m * k
        return 0

    lax.fori_loop(0, chunks, prepare, 0)

    lane = lax.broadcasted_iota(jnp.int32, (height, LANES), 1)

    def over_planes(body):
        def step(p, _):
            body(p)
            return 0
        lax.fori_loop(0, planes, step, 0, unroll=True)

    def beside(i, c, p, halo=True):
        mid = V[i, c, p + 1, rows, :]
        before = V[i, c - 1, p + 1, rows, :] if c > 0 else flat
        after = V[i, c + 1, p + 1, rows, :] if c < chunks - 1 else flat
        total = V[i, c, p + 1, pl.ds(PAD - 1, height), :]
        if halo or p > 0:
            total = total + V[i, c, p, rows, :]
        if halo or p < planes - 1:
            total = total + V[i, c, p + 2, rows, :]
        total = total + V[i, c, p + 1, pl.ds(PAD + 1, height), :]
        total = total + pltpu.roll(jnp.where(lane == LANES - 1, before, mid), 1, 1)
        total = total + pltpu.roll(jnp.where(lane == 0, after, mid), LANES - 1, 1)
        return mid, total

    def steps_before(e, c, p):
        z = ZB[e, c, p]
        both = 2.0 * XB[e, c, p] - 0.5 * z
        return jnp.where(even, z, both) if WAY[e][c] == "X" else both

    waited = set()

    def second(e, c):
        with scope(f"S{e}_{c}"):
            if WAY[e][c] == "X":
                @pl.when(even)
                def _():
                    landed(XB.at[e, c], xr.at[e, c])

                    def mix(p):
                        CB[e, c, p] = 2.0 * XB[e, c, p] - 0.5 * V[2 * e, c, p + 1, rows, :]
                    over_planes(mix)
                    z_copy(e, c, CB.at[e, c]).start()
            else:
                @pl.when(odd)
                def _():
                    if (e, c) not in waited:
                        landed(ZB.at[e, c], zr.at[e, c])
                    x_copy(e, c, ZB.at[e, c]).start()
                waited.add((e, c))

    def direct(e, c):
        with scope("direct"):
            @pl.when(odd)
            def _():
                if (e, c) == first_direct:
                    pl.semaphore_wait(token_d, 1)
                pltpu.make_async_remote_copy(
                    value(e, c), XB.at[e, c], xs, xr.at[e, c],
                    device_id={"tm": next_up}, device_id_type=MESH).start()

    def ready(e, c):
        with scope(f"R{e}_{c}"):
            if WAY[e][c] == "X":
                landed(ZB.at[e, c], zr.at[e, c])

                @pl.when(odd)
                def _():
                    landed(XB.at[e, c], xr.at[e, c])
            elif WAY[e][c] == "Z":
                landed(XB.at[e, c], xr.at[e, c])
                if (e, c) in waited:
                    @pl.when(even)
                    def _():
                        landed(ZB.at[e, c], zr.at[e, c])
                else:
                    landed(ZB.at[e, c], zr.at[e, c])
                    waited.add((e, c))
            else:
                landed(XB.at[e, c], xr.at[e, c])
                landed(ZB.at[e, c], zr.at[e, c])

    def sweep_first(e, c):
        with scope(f"H{e}_{c}"):
            if e > 0:
                wait_halo(2 * e, c)
            elif c == FIRST_SWEPT:
                wait_halo(0, 0)

        with scope(f"a{e}_{c}"):
            def early(p):
                mid, total = beside(2 * e, c, p)
                V[2 * e + 1, c, p + 1, rows, :] = FW[c, p] + KW[c, p] * total
            over_planes(early)
        ready(e, c)
        with scope(f"A{e}_{c}"):
            def step(p):
                g = W[c, p] * steps_before(e, c, p)
                G[c, p] = FW[c, p] + g
                V[2 * e + 1, c, p + 1, rows, :] = V[2 * e + 1, c, p + 1, rows, :] + g
            over_planes(step)
        send_halo(2 * e + 1, c)

    def sweep_second(e, c):
        n = e + 1
        i = 2 * e + 1

        def put(p, v):
            V[2 * n, c, p + 1, rows, :] = v
            if n == ITERS:
                p_out[0, p, :, lanes(c)] = v

        with scope(f"b{e}_{c}"):
            for p in range(planes):
                mid, total = beside(i, c, p, halo=False)
                v = G[c, p] + KW[c, p] * total
                if p in (0, planes - 1):
                    V[2 * n, c, p + 1, rows, :] = v
                else:
                    put(p, v)
        with scope(f"h{e}_{c}"):
            wait_halo(i, c)
        with scope(f"B{e}_{c}"):
            for p, beyond in ((0, 0), (planes - 1, planes + 1)):
                put(p, V[2 * n, c, p + 1, rows, :] + KW[c, p] * V[i, c, beyond, rows, :])

        @pl.when(even)
        def _():
            x_copy(n, c, value(n, c)).start()
        send_halo(2 * n, c)

    def even_z(e, c):
        @pl.when(even)
        def _():
            z_copy(e, c, value(e, c)).start()

    def odd_z(e, c):
        @pl.when(odd)
        def _():
            z_copy(e, c, value(e, c)).start()

    def own_x(e, c):
        @pl.when(odd)
        def _():
            x_copy(e, c, value(e, c)).start()

    def partial(e, c):
        with scope(f"Hl_{c}"):
            wait_halo(last, c)

        with scope(f"P_{c}"):
            def step(p):
                mid, total = beside(last, c, p)
                m = M[p, :, lanes(c)].astype(jnp.float32)
                G[c, p] = m * F[p, :, lanes(c)] - MD[c, p] * mid + MK[c, p] * total
            over_planes(step)

    def complete(e, c):
        ready(e, c)
        with scope(f"C_{c}"):
            def step(p):
                m = M[p, :, lanes(c)].astype(jnp.float32)
                r_out[0, p, :, lanes(c)] = G[c, p] + m * steps_before(ITERS, c, p)
            over_planes(step)

    acts = dict(S=second, A=sweep_first, B=sweep_second, E=even_z, O=odd_z, X=own_x, D=direct, P=partial, C=complete)
    relayed = next(c for name, e, c in STEPS if name == "A" and WAY[0][c] == "Z")
    first_direct = next(((e, c) for name, e, c in STEPS if name == "D"), None)
    for name, e, c in STEPS:
        acts[name](e, c)
        if first_direct and (name, e, c) == ("A", 0, relayed):
            answer(even, token_d, {"tm": prior})

    with scope("drain"):
        left(ZB, zs)
        left(XB, xs)
        for nb, at in ((2, inner), (1, jnp.logical_not(inner))):
            @pl.when(at)
            def _(nb=nb):
                left(V.at[:, :, pl.ds(0, nb), rows], hs)


def write_out(p_ref, r_ref, p_out, r_out, sem):
    copies = [
        pltpu.make_async_copy(src, dst, sem.at[i])
        for i, (src, dst) in enumerate(((p_ref, p_out), (r_ref, r_out)))
    ]
    for copy in copies:
        copy.start()
    for copy in copies:
        copy.wait()


def solution(mesh):
    n_tm, n_space = mesh.shape["tm"], mesh.shape["space"]
    placed = (
        P("tm", "space", None, None),
        P("tm", "space", None, None),
        P("space", None, None),
        P("tm", "space", None, None),
    )

    def body(forcing, inv_density, wall_mask, guess):
        planes, height, width = wall_mask.shape
        chunks = width // LANES
        full = (planes, height, width)
        cut = (chunks, planes, height, LANES)
        exchanges = ITERS + 1
        values = 2 * ITERS + 1
        f32 = jnp.float32
        pressure, residual = pl.pallas_call(
            functools.partial(kernel, n_tm, n_space),
            out_shape=[pltpu.VMEM(guess.shape, f32)] * 2,
            in_specs=[pl.BlockSpec(memory_space=pl.ANY)] * 4,
            out_specs=[pl.BlockSpec(memory_space=pltpu.VMEM)] * 2,
            scratch_shapes=[
                pltpu.VMEM((values, chunks, planes + 2, height + 2 * PAD, LANES), f32),
                pltpu.VMEM((exchanges,) + cut, f32),
                pltpu.VMEM((exchanges,) + cut, f32),
                pltpu.VMEM((exchanges,) + cut, f32),
                pltpu.VMEM(full, f32),
                pltpu.VMEM(full, inv_density.dtype),
                pltpu.VMEM(full, wall_mask.dtype),
                pltpu.VMEM(cut, f32),
                pltpu.VMEM(cut, f32),
                pltpu.VMEM(cut, f32),
                pltpu.VMEM(cut, f32),
                pltpu.VMEM(cut, f32),
                pltpu.VMEM(cut, f32),
                pltpu.SemaphoreType.DMA((4,)),
                pltpu.SemaphoreType.DMA,
                pltpu.SemaphoreType.DMA((exchanges, chunks)),
                pltpu.SemaphoreType.DMA,
                pltpu.SemaphoreType.DMA((exchanges, chunks)),
                pltpu.SemaphoreType.DMA,
                pltpu.SemaphoreType.DMA((2, chunks)),
                pltpu.SemaphoreType.DMA,
                pltpu.SemaphoreType.REGULAR,
                pltpu.SemaphoreType.REGULAR,
                pltpu.SemaphoreType.REGULAR,
                pltpu.SemaphoreType.REGULAR,
            ],
            compiler_params=pltpu.CompilerParams(collective_id=0, has_side_effects=True),
        )(forcing, inv_density, wall_mask, guess)
        return pl.pallas_call(
            write_out,
            out_shape=(jax.ShapeDtypeStruct(guess.shape, f32),) * 2,
            in_specs=[pl.BlockSpec(memory_space=pltpu.VMEM)] * 2,
            out_specs=(pl.BlockSpec(memory_space=pl.ANY),) * 2,
            scratch_shapes=[pltpu.SemaphoreType.DMA((2,))],
        )(*[pltpu.with_memory_space_constraint(v, pltpu.VMEM) for v in (pressure, residual)])

    return jax.shard_map(
        body,
        mesh=mesh,
        in_specs=placed,
        out_specs=(P("tm", "space", None, None), P("tm", "space", None, None)),
        check_vma=False,
    )
```

```python
import functools

import jax
import jax.numpy as jnp
from jax import lax
from jax.experimental import pallas as pl
from jax.experimental.pallas import tpu as pltpu
from jax.sharding import PartitionSpec as P

ITERS = 2
LANES = 128
PAD = 8
MESH = pl.DeviceIdType.MESH
FIRST_EVEN = (2, 4, 0)
FIRST_ODD = (0, 2, 1, 4, 3, 6, 5, 7)
FIRST_X = (1, 3, 5, 7)
WAY = ("ZXZXZXZX", "ZXZXZXZX", "ZZZXDXXZ")
STEPS = (
    ("S", 0, 1), ("S", 0, 3), ("S", 0, 5), ("S", 0, 0), ("S", 0, 7), ("E", 0, 6), ("S", 0, 2), ("A", 0, 1),
    ("A", 0, 0), ("A", 0, 2), ("B", 0, 0), ("E", 1, 0), ("S", 0, 4), ("O", 1, 0), ("B", 0, 1), ("X", 1, 1),
    ("A", 0, 3), ("B", 0, 2), ("O", 1, 1), ("E", 1, 2), ("A", 0, 4), ("S", 0, 6), ("A", 0, 5), ("S", 1, 1),
    ("B", 0, 3), ("X", 1, 3), ("B", 0, 4), ("E", 1, 4), ("O", 1, 2), ("A", 0, 6), ("A", 0, 7), ("B", 0, 5),
    ("X", 1, 5), ("O", 1, 3), ("S", 1, 3), ("B", 0, 6), ("E", 1, 6), ("S", 1, 5), ("O", 1, 4), ("O", 1, 6),
    ("B", 0, 7), ("S", 1, 0), ("A", 1, 1), ("X", 1, 7), ("A", 1, 0), ("S", 1, 2), ("O", 1, 5), ("S", 1, 7),
    ("B", 1, 0), ("A", 1, 2), ("E", 2, 0), ("A", 1, 3), ("B", 1, 1), ("E", 2, 1), ("O", 1, 7), ("O", 2, 1),
    ("S", 1, 4), ("S", 1, 6), ("A", 1, 4), ("B", 1, 2), ("E", 2, 2), ("P", 2, 0), ("O", 2, 0), ("B", 1, 3),
    ("X", 2, 3), ("A", 1, 6), ("A", 1, 5), ("S", 2, 3), ("P", 2, 1), ("O", 2, 2), ("A", 1, 7), ("B", 1, 6),
    ("X", 2, 6), ("B", 1, 4), ("B", 1, 5), ("D", 2, 4), ("X", 2, 5), ("E", 2, 4), ("B", 1, 7), ("O", 2, 7),
    ("E", 2, 7), ("S", 2, 1), ("S", 2, 0), ("O", 2, 6), ("O", 2, 3), ("S", 2, 6), ("S", 2, 2), ("P", 2, 2),
    ("S", 2, 5), ("C", 2, 2), ("P", 2, 5), ("P", 2, 4), ("P", 2, 6), ("C", 2, 1), ("P", 2, 3), ("O", 2, 4),
    ("S", 2, 7), ("C", 2, 0), ("O", 2, 5), ("P", 2, 7), ("C", 2, 3), ("C", 2, 4), ("C", 2, 7), ("C", 2, 6),
    ("C", 2, 5),
)
FIRST_SWEPT = next(c for name, e, c in STEPS if name == "A")


def kernel(
    n_tm, n_space,
    f_hbm, k_hbm, m_hbm, g_hbm, p_out, r_out,
    V, ZB, XB, CB, F, K, M, W, FW, KW, MD, MK, G,
    load_sem, zs, zr, xs, xr, hs, hr, h0, token_x, token_s, token_z, token_d,
):
    planes, height, width = F.shape
    chunks = width // LANES
    last = 2 * ITERS
    t = lax.axis_index("tm")
    s = lax.axis_index("space")
    even = lax.rem(t, 2) == 0
    odd = lax.rem(t, 2) == 1
    s_even = lax.rem(s, 2) == 0
    s_odd = lax.rem(s, 2) == 1
    partner = t + 1 - 2 * lax.rem(t, 2)
    ahead = lax.rem(t + 2, n_tm)
    behind = lax.rem(t + n_tm - 2, n_tm)
    next_up = lax.rem(t + 1, n_tm)
    prior = lax.rem(t + n_tm - 1, n_tm)
    has_lo = s > 0
    has_hi = s < n_space - 1
    inner = has_lo & has_hi
    rows = pl.ds(PAD, height)
    mine = pl.ds(1, planes)

    def lanes(c):
        return pl.ds(c * LANES, LANES)

    def scope(name):
        return jax.named_scope(name)

    load_g = [
        pltpu.make_async_copy(g_hbm.at[0, :, :, lanes(c)], V.at[0, c, mine, rows], load_sem.at[0])
        for c in range(chunks)
    ]
    loads = [
        pltpu.make_async_copy(k_hbm.at[0], K, load_sem.at[1]),
        pltpu.make_async_copy(m_hbm, M, load_sem.at[2]),
        pltpu.make_async_copy(f_hbm.at[0], F, load_sem.at[3]),
    ]

    barrier = pltpu.get_barrier_semaphore()
    first_z = t < 2
    last_z = t >= n_tm - 2
    near_z = (t >= n_tm - 4) & jnp.logical_not(last_z)
    by_token = t < n_tm - 4

    def greet(at, other):
        @pl.when(at)
        def _():
            pl.semaphore_signal(barrier, inc=1, device_id=other, device_id_type=MESH)

    def answer(at, token, other):
        @pl.when(at)
        def _():
            pl.semaphore_signal(token, inc=1, device_id=other, device_id_type=MESH)

    greet(first_z | last_z, {"tm": behind})
    greet(by_token, {"tm": ahead})
    greet(even, {"tm": partner})
    greet(s_odd, {"space": s - 1})
    greet(s_odd & has_hi, {"space": s + 1})

    for load in load_g + loads:
        load.start()

    one = jnp.int32(1)
    none = jnp.int32(0)
    told = jnp.where(first_z | last_z, none, one) + jnp.where(last_z | near_z, one, none) + jnp.where(odd, one, none)
    told = told + jnp.where(s_even & has_lo, one, none) + jnp.where(s_even & has_hi, one, none)
    with scope("bar"):
        for n in range(1, 6):
            @pl.when(told == n)
            def _(n=n):
                pl.semaphore_wait(barrier, n)
    answer(jnp.logical_not(first_z | last_z), token_z, {"tm": behind})
    answer(odd, token_x, {"tm": partner})
    answer(s_even & has_lo, token_s, {"space": s - 1})
    answer(s_even & has_hi, token_s, {"space": s + 1})

    def value(e, c):
        if e == 0:
            return g_hbm.at[0, :, :, lanes(c)]
        return V.at[2 * e, c, mine, rows]

    def plane(i, c, p):
        if i == 0:
            return g_hbm.at[0, p, :, lanes(c)]
        return V.at[i, c, 1 + p, rows]

    def z_copy(e, c, src):
        return pltpu.make_async_remote_copy(
            src, ZB.at[e, c], zs, zr.at[e, c], device_id={"tm": ahead}, device_id_type=MESH)

    def x_copy(e, c, src):
        return pltpu.make_async_remote_copy(
            src, XB.at[e, c], xs, xr.at[e, c], device_id={"tm": partner}, device_id_type=MESH)

    def halo_sem(i, c):
        return h0 if i == 0 else hr.at[(i - 1) % 2, c]

    def to_lo(i, c):
        return pltpu.make_async_remote_copy(
            plane(i, c, 0), V.at[i, c, planes + 1, rows], hs, halo_sem(i, c),
            device_id={"space": s - 1}, device_id_type=MESH)

    def to_hi(i, c):
        return pltpu.make_async_remote_copy(
            plane(i, c, planes - 1), V.at[i, c, 0, rows], hs, halo_sem(i, c),
            device_id={"space": s + 1}, device_id_type=MESH)

    def send_halo(i, c):
        @pl.when(has_lo)
        def _():
            to_lo(i, c).start()

        @pl.when(has_hi)
        def _():
            to_hi(i, c).start()

    def landed(ref, sem):
        pltpu.make_async_remote_copy(
            ref, ref, hs, sem, device_id={"tm": partner}, device_id_type=MESH).wait_recv()

    def left(ref, sem):
        pltpu.make_async_remote_copy(
            ref, ref, sem, h0, device_id={"tm": partner}, device_id_type=MESH).wait_send()

    def wait_halo(i, c):
        which = pl.ds(0, chunks) if i == 0 else pl.ds(c, 1)
        for nb, at in ((2, inner), (1, jnp.logical_not(inner))):
            @pl.when(at)
            def _(nb=nb):
                landed(V.at[i, which, pl.ds(0, nb), rows], halo_sem(i, c))

    def first_halos():
        for c in range(chunks):
            send_halo(0, c)

    with scope("send0"):
        @pl.when(odd & jnp.logical_not(last_z))
        def _():
            for c in FIRST_X:
                x_copy(0, c, value(0, c)).start()

        @pl.when(s_even & jnp.logical_not(last_z))
        def _():
            first_halos()

        @pl.when(by_token)
        def _():
            pl.semaphore_wait(token_z, 1)

        @pl.when(even)
        def _():
            for c in FIRST_EVEN:
                z_copy(0, c, value(0, c)).start()

        @pl.when(odd)
        def _():
            for c in FIRST_ODD:
                z_copy(0, c, value(0, c)).start()

        @pl.when(odd & last_z)
        def _():
            for c in FIRST_X:
                x_copy(0, c, value(0, c)).start()

        @pl.when(s_even & last_z)
        def _():
            first_halos()

    with scope("token_x"):
        @pl.when(even)
        def _():
            pl.semaphore_wait(token_x, 1)
            for c in range(chunks):
                x_copy(0, c, value(0, c)).start()

    with scope("token_s"):
        @pl.when(s_odd & inner)
        def _():
            pl.semaphore_wait(token_s, 2)

        @pl.when(s_odd & jnp.logical_not(inner))
        def _():
            pl.semaphore_wait(token_s, 1)

        @pl.when(s_odd)
        def _():
            first_halos()

    edge = jnp.zeros((PAD, LANES), jnp.float32)
    flat = jnp.zeros((height, LANES), jnp.float32)

    def clear(c, _):
        for i in range(last + 1):
            for p in range(1, planes + 1):
                V[i, c, p, pl.ds(0, PAD), :] = edge
                V[i, c, p, pl.ds(PAD + height, PAD), :] = edge
        return 0

    def clear_plane(p):
        def body(c, _):
            for i in range(last + 1):
                V[i, c, p, rows, :] = flat
            return 0
        lax.fori_loop(0, chunks, body, 0)

    lax.fori_loop(0, chunks, clear, 0)

    @pl.when(jnp.logical_not(has_lo))
    def _():
        clear_plane(0)

    @pl.when(jnp.logical_not(has_hi))
    def _():
        clear_plane(planes + 1)

    with scope("loads"):
        pltpu.make_async_copy(V.at[0, :, mine, rows], V.at[0, :, mine, rows], load_sem.at[0]).wait()
        for load in loads:
            load.wait()

    def prepare(c, _):
        at = pl.ds(pl.multiple_of(c * LANES, LANES), LANES)
        for p in range(planes):
            k = K[p, :, at].astype(jnp.float32)
            m = M[p, :, at].astype(jnp.float32)
            d = 1.5 + 6.0 * k
            w = m / d
            W[c, p] = w
            FW[c, p] = w * F[p, :, at]
            KW[c, p] = k * w
            MD[c, p] = m * d
            MK[c, p] = m * k
        return 0

    lax.fori_loop(0, chunks, prepare, 0)

    lane = lax.broadcasted_iota(jnp.int32, (height, LANES), 1)

    def over_planes(body):
        def step(p, _):
            body(p)
            return 0
        lax.fori_loop(0, planes, step, 0, unroll=True)

    def beside(i, c, p, halo=True):
        mid = V[i, c, p + 1, rows, :]
        before = V[i, c - 1, p + 1, rows, :] if c > 0 else flat
        after = V[i, c + 1, p + 1, rows, :] if c < chunks - 1 else flat
        total = V[i, c, p + 1, pl.ds(PAD - 1, height), :]
        if halo or p > 0:
            total = total + V[i, c, p, rows, :]
        if halo or p < planes - 1:
            total = total + V[i, c, p + 2, rows, :]
        total = total + V[i, c, p + 1, pl.ds(PAD + 1, height), :]
        total = total + pltpu.roll(jnp.where(lane == LANES - 1, before, mid), 1, 1)
        total = total + pltpu.roll(jnp.where(lane == 0, after, mid), LANES - 1, 1)
        return mid, total

    def steps_before(e, c, p):
        z = ZB[e, c, p]
        both = 2.0 * XB[e, c, p] - 0.5 * z
        return jnp.where(even, z, both) if WAY[e][c] == "X" else both

    waited = set()

    def second(e, c):
        with scope(f"S{e}_{c}"):
            if WAY[e][c] == "X":
                @pl.when(even)
                def _():
                    landed(XB.at[e, c], xr.at[e, c])

                    def mix(p):
                        CB[e, c, p] = 2.0 * XB[e, c, p] - 0.5 * V[2 * e, c, p + 1, rows, :]
                    over_planes(mix)
                    z_copy(e, c, CB.at[e, c]).start()
            else:
                @pl.when(odd)
                def _():
                    if (e, c) not in waited:
                        landed(ZB.at[e, c], zr.at[e, c])
                    x_copy(e, c, ZB.at[e, c]).start()
                waited.add((e, c))

    def direct(e, c):
        with scope("direct"):
            @pl.when(odd)
            def _():
                if (e, c) == first_direct:
                    pl.semaphore_wait(token_d, 1)
                pltpu.make_async_remote_copy(
                    value(e, c), XB.at[e, c], xs, xr.at[e, c],
                    device_id={"tm": next_up}, device_id_type=MESH).start()

    def ready(e, c):
        with scope(f"R{e}_{c}"):
            if WAY[e][c] == "X":
                landed(ZB.at[e, c], zr.at[e, c])

                @pl.when(odd)
                def _():
                    landed(XB.at[e, c], xr.at[e, c])
            elif WAY[e][c] == "Z":
                landed(XB.at[e, c], xr.at[e, c])
                if (e, c) in waited:
                    @pl.when(even)
                    def _():
                        landed(ZB.at[e, c], zr.at[e, c])
                else:
                    landed(ZB.at[e, c], zr.at[e, c])
                    waited.add((e, c))
            else:
                landed(XB.at[e, c], xr.at[e, c])
                landed(ZB.at[e, c], zr.at[e, c])

    def sweep_first(e, c):
        with scope(f"H{e}_{c}"):
            if e > 0:
                wait_halo(2 * e, c)
            elif c == FIRST_SWEPT:
                wait_halo(0, 0)

        with scope(f"a{e}_{c}"):
            def early(p):
                mid, total = beside(2 * e, c, p)
                V[2 * e + 1, c, p + 1, rows, :] = FW[c, p] + KW[c, p] * total
            over_planes(early)
        ready(e, c)
        with scope(f"A{e}_{c}"):
            def step(p):
                g = W[c, p] * steps_before(e, c, p)
                G[c, p] = FW[c, p] + g
                V[2 * e + 1, c, p + 1, rows, :] = V[2 * e + 1, c, p + 1, rows, :] + g
            over_planes(step)
        send_halo(2 * e + 1, c)

    def sweep_second(e, c):
        n = e + 1
        i = 2 * e + 1

        def put(p, v):
            V[2 * n, c, p + 1, rows, :] = v
            if n == ITERS:
                p_out[0, p, :, lanes(c)] = v

        with scope(f"b{e}_{c}"):
            for p in range(planes):
                mid, total = beside(i, c, p, halo=False)
                v = G[c, p] + KW[c, p] * total
                if p in (0, planes - 1):
                    V[2 * n, c, p + 1, rows, :] = v
                else:
                    put(p, v)
        with scope(f"h{e}_{c}"):
            wait_halo(i, c)
        with scope(f"B{e}_{c}"):
            for p, beyond in ((0, 0), (planes - 1, planes + 1)):
                put(p, V[2 * n, c, p + 1, rows, :] + KW[c, p] * V[i, c, beyond, rows, :])

        @pl.when(even)
        def _():
            x_copy(n, c, value(n, c)).start()
        send_halo(2 * n, c)

    def even_z(e, c):
        @pl.when(even)
        def _():
            z_copy(e, c, value(e, c)).start()

    def odd_z(e, c):
        @pl.when(odd)
        def _():
            z_copy(e, c, value(e, c)).start()

    def own_x(e, c):
        @pl.when(odd)
        def _():
            x_copy(e, c, value(e, c)).start()

    def partial(e, c):
        with scope(f"Hl_{c}"):
            wait_halo(last, c)

        with scope(f"P_{c}"):
            def step(p):
                mid, total = beside(last, c, p)
                m = M[p, :, lanes(c)].astype(jnp.float32)
                G[c, p] = m * F[p, :, lanes(c)] - MD[c, p] * mid + MK[c, p] * total
            over_planes(step)

    def complete(e, c):
        ready(e, c)
        with scope(f"C_{c}"):
            def step(p):
                m = M[p, :, lanes(c)].astype(jnp.float32)
                r_out[0, p, :, lanes(c)] = G[c, p] + m * steps_before(ITERS, c, p)
            over_planes(step)

    acts = dict(S=second, A=sweep_first, B=sweep_second, E=even_z, O=odd_z, X=own_x, D=direct, P=partial, C=complete)
    relayed = next(c for name, e, c in STEPS if name == "A" and WAY[0][c] == "Z")
    first_direct = next(((e, c) for name, e, c in STEPS if name == "D"), None)
    for name, e, c in STEPS:
        acts[name](e, c)
        if first_direct and (name, e, c) == ("A", 0, relayed):
            answer(even, token_d, {"tm": prior})

    with scope("drain"):
        left(ZB, zs)
        left(XB, xs)
        for nb, at in ((2, inner), (1, jnp.logical_not(inner))):
            @pl.when(at)
            def _(nb=nb):
                left(V.at[:, :, pl.ds(0, nb), rows], hs)


def write_out(p_ref, r_ref, p_out, r_out, sem):
    copies = [
        pltpu.make_async_copy(src, dst, sem.at[i])
        for i, (src, dst) in enumerate(((p_ref, p_out), (r_ref, r_out)))
    ]
    for copy in copies:
        copy.start()
    for copy in copies:
        copy.wait()


def solution(mesh):
    n_tm, n_space = mesh.shape["tm"], mesh.shape["space"]
    placed = (
        P("tm", "space", None, None),
        P("tm", "space", None, None),
        P("space", None, None),
        P("tm", "space", None, None),
    )

    def body(forcing, inv_density, wall_mask, guess):
        planes, height, width = wall_mask.shape
        chunks = width // LANES
        full = (planes, height, width)
        cut = (chunks, planes, height, LANES)
        exchanges = ITERS + 1
        values = 2 * ITERS + 1
        f32 = jnp.float32
        pressure, residual = pl.pallas_call(
            functools.partial(kernel, n_tm, n_space),
            out_shape=[pltpu.VMEM(guess.shape, f32)] * 2,
            in_specs=[pl.BlockSpec(memory_space=pl.ANY)] * 4,
            out_specs=[pl.BlockSpec(memory_space=pltpu.VMEM)] * 2,
            scratch_shapes=[
                pltpu.VMEM((values, chunks, planes + 2, height + 2 * PAD, LANES), f32),
                pltpu.VMEM((exchanges,) + cut, f32),
                pltpu.VMEM((exchanges,) + cut, f32),
                pltpu.VMEM((exchanges,) + cut, f32),
                pltpu.VMEM(full, f32),
                pltpu.VMEM(full, inv_density.dtype),
                pltpu.VMEM(full, wall_mask.dtype),
                pltpu.VMEM(cut, f32),
                pltpu.VMEM(cut, f32),
                pltpu.VMEM(cut, f32),
                pltpu.VMEM(cut, f32),
                pltpu.VMEM(cut, f32),
                pltpu.VMEM(cut, f32),
                pltpu.SemaphoreType.DMA((4,)),
                pltpu.SemaphoreType.DMA,
                pltpu.SemaphoreType.DMA((exchanges, chunks)),
                pltpu.SemaphoreType.DMA,
                pltpu.SemaphoreType.DMA((exchanges, chunks)),
                pltpu.SemaphoreType.DMA,
                pltpu.SemaphoreType.DMA((2, chunks)),
                pltpu.SemaphoreType.DMA,
                pltpu.SemaphoreType.REGULAR,
                pltpu.SemaphoreType.REGULAR,
                pltpu.SemaphoreType.REGULAR,
                pltpu.SemaphoreType.REGULAR,
            ],
            compiler_params=pltpu.CompilerParams(collective_id=0, has_side_effects=True),
        )(forcing, inv_density, wall_mask, guess)
        return pl.pallas_call(
            write_out,
            out_shape=(jax.ShapeDtypeStruct(guess.shape, f32),) * 2,
            in_specs=[pl.BlockSpec(memory_space=pltpu.VMEM)] * 2,
            out_specs=(pl.BlockSpec(memory_space=pl.ANY),) * 2,
            scratch_shapes=[pltpu.SemaphoreType.DMA((2,))],
        )(*[pltpu.with_memory_space_constraint(v, pltpu.VMEM) for v in (pressure, residual)])

    return jax.shard_map(
        body,
        mesh=mesh,
        in_specs=placed,
        out_specs=(P("tm", "space", None, None), P("tm", "space", None, None)),
        check_vma=False,
    )
```

```python
import functools

import jax
import jax.numpy as jnp
from jax import lax
from jax.experimental import pallas as pl
from jax.experimental.pallas import tpu as pltpu
from jax.sharding import PartitionSpec as P

ITERS = 2
LANES = 128
PAD = 8
MESH = pl.DeviceIdType.MESH
FIRST_EVEN = (2, 4, 0)
FIRST_ODD = (0, 2, 1, 4, 3, 6, 5, 7)
FIRST_X = (1, 3, 5, 7)
WAY = ("ZXZXZXZX", "ZXZXZXZX", "ZZZXDXXZ")
STEPS = (
    ("S", 0, 1), ("S", 0, 3), ("S", 0, 5), ("S", 0, 0), ("S", 0, 7), ("E", 0, 6), ("S", 0, 2), ("A", 0, 1),
    ("A", 0, 0), ("A", 0, 2), ("B", 0, 0), ("E", 1, 0), ("S", 0, 4), ("O", 1, 0), ("B", 0, 1), ("X", 1, 1),
    ("A", 0, 3), ("B", 0, 2), ("O", 1, 1), ("E", 1, 2), ("A", 0, 4), ("S", 0, 6), ("A", 0, 5), ("S", 1, 1),
    ("B", 0, 3), ("X", 1, 3), ("B", 0, 4), ("E", 1, 4), ("O", 1, 2), ("A", 0, 6), ("A", 0, 7), ("B", 0, 5),
    ("X", 1, 5), ("O", 1, 3), ("S", 1, 3), ("B", 0, 6), ("E", 1, 6), ("S", 1, 5), ("O", 1, 4), ("O", 1, 6),
    ("B", 0, 7), ("S", 1, 0), ("A", 1, 1), ("X", 1, 7), ("A", 1, 0), ("S", 1, 2), ("O", 1, 5), ("S", 1, 7),
    ("B", 1, 0), ("A", 1, 2), ("E", 2, 0), ("A", 1, 3), ("B", 1, 1), ("E", 2, 1), ("O", 1, 7), ("O", 2, 1),
    ("S", 1, 4), ("S", 1, 6), ("A", 1, 4), ("B", 1, 2), ("E", 2, 2), ("P", 2, 0), ("O", 2, 0), ("B", 1, 3),
    ("X", 2, 3), ("A", 1, 6), ("A", 1, 5), ("S", 2, 3), ("P", 2, 1), ("O", 2, 2), ("A", 1, 7), ("B", 1, 6),
    ("X", 2, 6), ("B", 1, 4), ("B", 1, 5), ("D", 2, 4), ("X", 2, 5), ("E", 2, 4), ("B", 1, 7), ("O", 2, 7),
    ("E", 2, 7), ("S", 2, 1), ("S", 2, 0), ("O", 2, 6), ("O", 2, 3), ("S", 2, 6), ("S", 2, 2), ("P", 2, 2),
    ("S", 2, 5), ("C", 2, 2), ("P", 2, 5), ("P", 2, 4), ("P", 2, 6), ("C", 2, 1), ("P", 2, 3), ("O", 2, 4),
    ("S", 2, 7), ("C", 2, 0), ("O", 2, 5), ("P", 2, 7), ("C", 2, 3), ("C", 2, 4), ("C", 2, 7), ("C", 2, 6),
    ("C", 2, 5),
)
FIRST_SWEPT = next(c for name, e, c in STEPS if name == "A")


def kernel(
    n_tm, n_space,
    f_hbm, k_hbm, m_hbm, g_hbm, p_out, r_out,
    V, ZB, XB, CB, F, K, M, W, FW, KW, MD, MK, G,
    load_sem, zs, xs, got, hs, hr, h0, token_x, token_s, token_z, token_d,
):
    planes, height, width = F.shape
    chunks = width // LANES
    last = 2 * ITERS
    t = lax.axis_index("tm")
    s = lax.axis_index("space")
    even = lax.rem(t, 2) == 0
    odd = lax.rem(t, 2) == 1
    s_even = lax.rem(s, 2) == 0
    s_odd = lax.rem(s, 2) == 1
    partner = t + 1 - 2 * lax.rem(t, 2)
    ahead = lax.rem(t + 2, n_tm)
    behind = lax.rem(t + n_tm - 2, n_tm)
    next_up = lax.rem(t + 1, n_tm)
    prior = lax.rem(t + n_tm - 1, n_tm)
    has_lo = s > 0
    has_hi = s < n_space - 1
    inner = has_lo & has_hi
    rows = pl.ds(PAD, height)
    mine = pl.ds(1, planes)

    def lanes(c):
        return pl.ds(c * LANES, LANES)

    def scope(name):
        return jax.named_scope(name)

    load_g = [
        pltpu.make_async_copy(g_hbm.at[0, :, :, lanes(c)], V.at[0, c, mine, rows], load_sem.at[0])
        for c in range(chunks)
    ]
    loads = [
        pltpu.make_async_copy(k_hbm.at[0], K, load_sem.at[1]),
        pltpu.make_async_copy(m_hbm, M, load_sem.at[2]),
        pltpu.make_async_copy(f_hbm.at[0], F, load_sem.at[3]),
    ]

    barrier = pltpu.get_barrier_semaphore()
    first_z = t < 2
    last_z = t >= n_tm - 2
    near_z = (t >= n_tm - 4) & jnp.logical_not(last_z)
    by_token = t < n_tm - 4

    def greet(at, other):
        @pl.when(at)
        def _():
            pl.semaphore_signal(barrier, inc=1, device_id=other, device_id_type=MESH)

    def answer(at, token, other):
        @pl.when(at)
        def _():
            pl.semaphore_signal(token, inc=1, device_id=other, device_id_type=MESH)

    greet(first_z | last_z, {"tm": behind})
    greet(by_token, {"tm": ahead})
    greet(even, {"tm": partner})
    greet(s_odd, {"space": s - 1})
    greet(s_odd & has_hi, {"space": s + 1})

    for load in load_g + loads:
        load.start()

    one = jnp.int32(1)
    none = jnp.int32(0)
    told = jnp.where(first_z | last_z, none, one) + jnp.where(last_z | near_z, one, none) + jnp.where(odd, one, none)
    told = told + jnp.where(s_even & has_lo, one, none) + jnp.where(s_even & has_hi, one, none)
    with scope("bar"):
        for n in range(1, 6):
            @pl.when(told == n)
            def _(n=n):
                pl.semaphore_wait(barrier, n)
    answer(jnp.logical_not(first_z | last_z), token_z, {"tm": behind})
    answer(odd, token_x, {"tm": partner})
    answer(s_even & has_lo, token_s, {"space": s - 1})
    answer(s_even & has_hi, token_s, {"space": s + 1})

    def value(e, c):
        if e == 0:
            return g_hbm.at[0, :, :, lanes(c)]
        return V.at[2 * e, c, mine, rows]

    def plane(i, c, p):
        if i == 0:
            return g_hbm.at[0, p, :, lanes(c)]
        return V.at[i, c, 1 + p, rows]

    def alone(e, c, to_even):
        return WAY[e][c] == ("X" if to_even else "Z")

    def own_slot(e, c):
        return got.at[e, chunks + WAY[e][:c].count(WAY[e][c])]

    def z_got(e, c, to_even):
        return own_slot(e, c) if not to_even and alone(e, c, to_even) else got.at[e, c]

    def x_got(e, c, to_even):
        return own_slot(e, c) if to_even and alone(e, c, to_even) else got.at[e, c]

    def z_copy(e, c, src, to_even):
        return pltpu.make_async_remote_copy(
            src, ZB.at[e, c], zs, z_got(e, c, to_even), device_id={"tm": ahead}, device_id_type=MESH)

    def x_copy(e, c, src, to_even):
        return pltpu.make_async_remote_copy(
            src, XB.at[e, c], xs, x_got(e, c, to_even), device_id={"tm": partner}, device_id_type=MESH)

    def halo_sem(i, c):
        return h0 if i == 0 else hr.at[(i - 1) % 2, c]

    def to_lo(i, c):
        return pltpu.make_async_remote_copy(
            plane(i, c, 0), V.at[i, c, planes + 1, rows], hs, halo_sem(i, c),
            device_id={"space": s - 1}, device_id_type=MESH)

    def to_hi(i, c):
        return pltpu.make_async_remote_copy(
            plane(i, c, planes - 1), V.at[i, c, 0, rows], hs, halo_sem(i, c),
            device_id={"space": s + 1}, device_id_type=MESH)

    def send_halo(i, c):
        @pl.when(has_lo)
        def _():
            to_lo(i, c).start()

        @pl.when(has_hi)
        def _():
            to_hi(i, c).start()

    def landed(ref, sem):
        pltpu.make_async_remote_copy(
            ref, ref, hs, sem, device_id={"tm": partner}, device_id_type=MESH).wait_recv()

    def left(ref, sem):
        pltpu.make_async_remote_copy(
            ref, ref, sem, h0, device_id={"tm": partner}, device_id_type=MESH).wait_send()

    def wait_halo(i, c):
        which = pl.ds(0, chunks) if i == 0 else pl.ds(c, 1)
        for nb, at in ((2, inner), (1, jnp.logical_not(inner))):
            @pl.when(at)
            def _(nb=nb):
                landed(V.at[i, which, pl.ds(0, nb), rows], halo_sem(i, c))

    def first_halos():
        for c in range(chunks):
            send_halo(0, c)

    with scope("send0"):
        @pl.when(odd & jnp.logical_not(last_z))
        def _():
            for c in FIRST_X:
                x_copy(0, c, value(0, c), True).start()

        @pl.when(s_even & jnp.logical_not(last_z))
        def _():
            first_halos()

        @pl.when(by_token)
        def _():
            pl.semaphore_wait(token_z, 1)

        @pl.when(even)
        def _():
            for c in FIRST_EVEN:
                z_copy(0, c, value(0, c), True).start()

        @pl.when(odd)
        def _():
            for c in FIRST_ODD:
                z_copy(0, c, value(0, c), False).start()

        @pl.when(odd & last_z)
        def _():
            for c in FIRST_X:
                x_copy(0, c, value(0, c), True).start()

        @pl.when(s_even & last_z)
        def _():
            first_halos()

    with scope("token_x"):
        @pl.when(even)
        def _():
            pl.semaphore_wait(token_x, 1)
            for c in range(chunks):
                x_copy(0, c, value(0, c), False).start()

    with scope("token_s"):
        @pl.when(s_odd & inner)
        def _():
            pl.semaphore_wait(token_s, 2)

        @pl.when(s_odd & jnp.logical_not(inner))
        def _():
            pl.semaphore_wait(token_s, 1)

        @pl.when(s_odd)
        def _():
            first_halos()

    edge = jnp.zeros((PAD, LANES), jnp.float32)
    flat = jnp.zeros((height, LANES), jnp.float32)

    def clear(c, _):
        for i in range(last + 1):
            for p in range(1, planes + 1):
                V[i, c, p, pl.ds(0, PAD), :] = edge
                V[i, c, p, pl.ds(PAD + height, PAD), :] = edge
        return 0

    def clear_plane(p):
        def body(c, _):
            for i in range(last + 1):
                V[i, c, p, rows, :] = flat
            return 0
        lax.fori_loop(0, chunks, body, 0)

    lax.fori_loop(0, chunks, clear, 0)

    @pl.when(jnp.logical_not(has_lo))
    def _():
        clear_plane(0)

    @pl.when(jnp.logical_not(has_hi))
    def _():
        clear_plane(planes + 1)

    with scope("loads"):
        pltpu.make_async_copy(V.at[0, :, mine, rows], V.at[0, :, mine, rows], load_sem.at[0]).wait()
        for load in loads:
            load.wait()

    def prepare(c, _):
        at = pl.ds(pl.multiple_of(c * LANES, LANES), LANES)
        for p in range(planes):
            k = K[p, :, at].astype(jnp.float32)
            m = M[p, :, at].astype(jnp.float32)
            d = 1.5 + 6.0 * k
            w = m / d
            W[c, p] = w
            FW[c, p] = w * F[p, :, at]
            KW[c, p] = k * w
            MD[c, p] = m * d
            MK[c, p] = m * k
        return 0

    lax.fori_loop(0, chunks, prepare, 0)

    lane = lax.broadcasted_iota(jnp.int32, (height, LANES), 1)

    def over_planes(body):
        def step(p, _):
            body(p)
            return 0
        lax.fori_loop(0, planes, step, 0, unroll=True)

    def beside(i, c, p, halo=True):
        mid = V[i, c, p + 1, rows, :]
        before = V[i, c - 1, p + 1, rows, :] if c > 0 else flat
        after = V[i, c + 1, p + 1, rows, :] if c < chunks - 1 else flat
        total = V[i, c, p + 1, pl.ds(PAD - 1, height), :]
        if halo or p > 0:
            total = total + V[i, c, p, rows, :]
        if halo or p < planes - 1:
            total = total + V[i, c, p + 2, rows, :]
        total = total + V[i, c, p + 1, pl.ds(PAD + 1, height), :]
        total = total + pltpu.roll(jnp.where(lane == LANES - 1, before, mid), 1, 1)
        total = total + pltpu.roll(jnp.where(lane == 0, after, mid), LANES - 1, 1)
        return mid, total

    def steps_before(e, c, p):
        z = ZB[e, c, p]
        both = 2.0 * XB[e, c, p] - 0.5 * z
        return jnp.where(even, z, both) if WAY[e][c] == "X" else both

    waited = set()

    def second(e, c):
        with scope(f"S{e}_{c}"):
            if WAY[e][c] == "X":
                @pl.when(even)
                def _():
                    landed(XB.at[e, c], x_got(e, c, True))

                    def mix(p):
                        CB[e, c, p] = 2.0 * XB[e, c, p] - 0.5 * V[2 * e, c, p + 1, rows, :]
                    over_planes(mix)
                    z_copy(e, c, CB.at[e, c], True).start()
            else:
                @pl.when(odd)
                def _():
                    if (e, c) not in waited:
                        landed(ZB.at[e, c], z_got(e, c, False))
                    x_copy(e, c, ZB.at[e, c], True).start()
                waited.add((e, c))

    def direct(e, c):
        with scope("direct"):
            @pl.when(odd)
            def _():
                if (e, c) == first_direct:
                    pl.semaphore_wait(token_d, 1)
                pltpu.make_async_remote_copy(
                    value(e, c), XB.at[e, c], xs, x_got(e, c, True),
                    device_id={"tm": next_up}, device_id_type=MESH).start()

    def ready(e, c):
        with scope(f"R{e}_{c}"):
            pair = XB.at[e, pl.ds(0, 2)]
            if WAY[e][c] == "D":
                landed(pair, got.at[e, c])
                return
            for to_even, at in ((True, even), (False, odd)):
                @pl.when(at)
                def _(to_even=to_even):
                    if not alone(e, c, to_even):
                        landed(pair, got.at[e, c])
                        return
                    landed(ZB.at[e, c] if to_even else XB.at[e, c], got.at[e, c])
                    if not to_even and (e, c) not in waited:
                        landed(ZB.at[e, c], z_got(e, c, False))
            waited.add((e, c))

    def sweep_first(e, c):
        with scope(f"H{e}_{c}"):
            if e > 0:
                wait_halo(2 * e, c)
            elif c == FIRST_SWEPT:
                wait_halo(0, 0)

        with scope(f"a{e}_{c}"):
            def early(p):
                mid, total = beside(2 * e, c, p)
                V[2 * e + 1, c, p + 1, rows, :] = FW[c, p] + KW[c, p] * total
            over_planes(early)
        ready(e, c)
        with scope(f"A{e}_{c}"):
            def step(p):
                g = W[c, p] * steps_before(e, c, p)
                G[c, p] = FW[c, p] + g
                V[2 * e + 1, c, p + 1, rows, :] = V[2 * e + 1, c, p + 1, rows, :] + g
            over_planes(step)
        send_halo(2 * e + 1, c)

    def sweep_second(e, c):
        n = e + 1
        i = 2 * e + 1

        def put(p, v):
            V[2 * n, c, p + 1, rows, :] = v
            if n == ITERS:
                p_out[0, p, :, lanes(c)] = v

        with scope(f"b{e}_{c}"):
            for p in range(planes):
                mid, total = beside(i, c, p, halo=False)
                v = G[c, p] + KW[c, p] * total
                if p in (0, planes - 1):
                    V[2 * n, c, p + 1, rows, :] = v
                else:
                    put(p, v)
        with scope(f"h{e}_{c}"):
            wait_halo(i, c)
        with scope(f"B{e}_{c}"):
            for p, beyond in ((0, 0), (planes - 1, planes + 1)):
                put(p, V[2 * n, c, p + 1, rows, :] + KW[c, p] * V[i, c, beyond, rows, :])

        @pl.when(even)
        def _():
            x_copy(n, c, value(n, c), False).start()
        send_halo(2 * n, c)

    def even_z(e, c):
        @pl.when(even)
        def _():
            z_copy(e, c, value(e, c), True).start()

    def odd_z(e, c):
        @pl.when(odd)
        def _():
            z_copy(e, c, value(e, c), False).start()

    def own_x(e, c):
        @pl.when(odd)
        def _():
            x_copy(e, c, value(e, c), True).start()

    def partial(e, c):
        with scope(f"Hl_{c}"):
            wait_halo(last, c)

        with scope(f"P_{c}"):
            def step(p):
                mid, total = beside(last, c, p)
                m = M[p, :, lanes(c)].astype(jnp.float32)
                G[c, p] = m * F[p, :, lanes(c)] - MD[c, p] * mid + MK[c, p] * total
            over_planes(step)

    def complete(e, c):
        ready(e, c)
        with scope(f"C_{c}"):
            def step(p):
                m = M[p, :, lanes(c)].astype(jnp.float32)
                r_out[0, p, :, lanes(c)] = G[c, p] + m * steps_before(ITERS, c, p)
            over_planes(step)

    acts = dict(S=second, A=sweep_first, B=sweep_second, E=even_z, O=odd_z, X=own_x, D=direct, P=partial, C=complete)
    relayed = next(c for name, e, c in STEPS if name == "A" and WAY[0][c] == "Z")
    first_direct = next(((e, c) for name, e, c in STEPS if name == "D"), None)
    for name, e, c in STEPS:
        acts[name](e, c)
        if first_direct and (name, e, c) == ("A", 0, relayed):
            answer(even, token_d, {"tm": prior})

    with scope("drain"):
        left(ZB, zs)
        left(XB, xs)
        for nb, at in ((2, inner), (1, jnp.logical_not(inner))):
            @pl.when(at)
            def _(nb=nb):
                left(V.at[:, :, pl.ds(0, nb), rows], hs)


def write_out(p_ref, r_ref, p_out, r_out, sem):
    copies = [
        pltpu.make_async_copy(src, dst, sem.at[i])
        for i, (src, dst) in enumerate(((p_ref, p_out), (r_ref, r_out)))
    ]
    for copy in copies:
        copy.start()
    for copy in copies:
        copy.wait()


def solution(mesh):
    n_tm, n_space = mesh.shape["tm"], mesh.shape["space"]
    placed = (
        P("tm", "space", None, None),
        P("tm", "space", None, None),
        P("space", None, None),
        P("tm", "space", None, None),
    )

    def body(forcing, inv_density, wall_mask, guess):
        planes, height, width = wall_mask.shape
        chunks = width // LANES
        full = (planes, height, width)
        cut = (chunks, planes, height, LANES)
        exchanges = ITERS + 1
        values = 2 * ITERS + 1
        f32 = jnp.float32
        pressure, residual = pl.pallas_call(
            functools.partial(kernel, n_tm, n_space),
            out_shape=[pltpu.VMEM(guess.shape, f32)] * 2,
            in_specs=[pl.BlockSpec(memory_space=pl.ANY)] * 4,
            out_specs=[pl.BlockSpec(memory_space=pltpu.VMEM)] * 2,
            scratch_shapes=[
                pltpu.VMEM((values, chunks, planes + 2, height + 2 * PAD, LANES), f32),
                pltpu.VMEM((exchanges,) + cut, f32),
                pltpu.VMEM((exchanges,) + cut, f32),
                pltpu.VMEM((exchanges,) + cut, f32),
                pltpu.VMEM(full, f32),
                pltpu.VMEM(full, inv_density.dtype),
                pltpu.VMEM(full, wall_mask.dtype),
                pltpu.VMEM(cut, f32),
                pltpu.VMEM(cut, f32),
                pltpu.VMEM(cut, f32),
                pltpu.VMEM(cut, f32),
                pltpu.VMEM(cut, f32),
                pltpu.VMEM(cut, f32),
                pltpu.SemaphoreType.DMA((4,)),
                pltpu.SemaphoreType.DMA,
                pltpu.SemaphoreType.DMA,
                pltpu.SemaphoreType.DMA((exchanges, chunks + chunks // 2)),
                pltpu.SemaphoreType.DMA,
                pltpu.SemaphoreType.DMA((2, chunks)),
                pltpu.SemaphoreType.DMA,
                pltpu.SemaphoreType.REGULAR,
                pltpu.SemaphoreType.REGULAR,
                pltpu.SemaphoreType.REGULAR,
                pltpu.SemaphoreType.REGULAR,
            ],
            compiler_params=pltpu.CompilerParams(collective_id=0, has_side_effects=True),
        )(forcing, inv_density, wall_mask, guess)
        return pl.pallas_call(
            write_out,
            out_shape=(jax.ShapeDtypeStruct(guess.shape, f32),) * 2,
            in_specs=[pl.BlockSpec(memory_space=pltpu.VMEM)] * 2,
            out_specs=(pl.BlockSpec(memory_space=pl.ANY),) * 2,
            scratch_shapes=[pltpu.SemaphoreType.DMA((2,))],
        )(*[pltpu.with_memory_space_constraint(v, pltpu.VMEM) for v in (pressure, residual)])

    return jax.shard_map(
        body,
        mesh=mesh,
        in_specs=placed,
        out_specs=(P("tm", "space", None, None), P("tm", "space", None, None)),
        check_vma=False,
    )
```

```python
import functools

import jax
import jax.numpy as jnp
from jax import lax
from jax.experimental import pallas as pl
from jax.experimental.pallas import tpu as pltpu
from jax.sharding import PartitionSpec as P

ITERS = 2
LANES = 128
PAD = 8
MESH = pl.DeviceIdType.MESH
FIRST_EVEN = (2, 4, 0)
FIRST_ODD = (0, 2, 1, 4, 3, 6, 5, 7)
FIRST_X = (1, 3, 5, 7)
WAY = ("ZXZXZXZX", "ZXZXZXZX", "ZZZXDXXZ")
STEPS = (
    ("S", 0, 1), ("S", 0, 3), ("S", 0, 5), ("S", 0, 0), ("S", 0, 7), ("E", 0, 6), ("S", 0, 2), ("A", 0, 1),
    ("A", 0, 0), ("A", 0, 2), ("B", 0, 0), ("E", 1, 0), ("S", 0, 4), ("O", 1, 0), ("B", 0, 1), ("X", 1, 1),
    ("A", 0, 3), ("B", 0, 2), ("O", 1, 1), ("E", 1, 2), ("A", 0, 4), ("S", 0, 6), ("A", 0, 5), ("S", 1, 1),
    ("B", 0, 3), ("X", 1, 3), ("B", 0, 4), ("E", 1, 4), ("O", 1, 2), ("A", 0, 6), ("A", 0, 7), ("B", 0, 5),
    ("X", 1, 5), ("O", 1, 3), ("S", 1, 3), ("B", 0, 6), ("E", 1, 6), ("S", 1, 5), ("O", 1, 4), ("O", 1, 6),
    ("B", 0, 7), ("S", 1, 0), ("A", 1, 1), ("X", 1, 7), ("A", 1, 0), ("S", 1, 2), ("O", 1, 5), ("S", 1, 7),
    ("B", 1, 0), ("A", 1, 2), ("E", 2, 0), ("A", 1, 3), ("B", 1, 1), ("E", 2, 1), ("O", 1, 7), ("O", 2, 1),
    ("S", 1, 4), ("S", 1, 6), ("A", 1, 4), ("B", 1, 2), ("E", 2, 2), ("P", 2, 0), ("O", 2, 0), ("B", 1, 3),
    ("X", 2, 3), ("A", 1, 6), ("A", 1, 5), ("S", 2, 3), ("P", 2, 1), ("O", 2, 2), ("A", 1, 7), ("B", 1, 6),
    ("X", 2, 6), ("B", 1, 4), ("B", 1, 5), ("D", 2, 4), ("X", 2, 5), ("E", 2, 4), ("B", 1, 7), ("O", 2, 7),
    ("E", 2, 7), ("S", 2, 1), ("S", 2, 0), ("O", 2, 6), ("O", 2, 3), ("S", 2, 6), ("S", 2, 2), ("P", 2, 2),
    ("S", 2, 5), ("C", 2, 2), ("P", 2, 5), ("P", 2, 4), ("P", 2, 6), ("C", 2, 1), ("P", 2, 3), ("O", 2, 4),
    ("S", 2, 7), ("C", 2, 0), ("O", 2, 5), ("P", 2, 7), ("C", 2, 3), ("C", 2, 4), ("C", 2, 7), ("C", 2, 6),
    ("C", 2, 5),
)
FIRST_SWEPT = next(c for name, e, c in STEPS if name == "A")


def kernel(
    n_tm, n_space,
    f_hbm, k_hbm, m_hbm, g_hbm, p_out, r_out,
    V, ZB, XB, CB, F, K, M, W, FW, KW, MD, MK, G,
    load_sem, zs, xs, got, hs, hr, h0, token_x, token_s, token_z, token_d,
):
    planes, height, width = F.shape
    chunks = width // LANES
    last = 2 * ITERS
    t = lax.axis_index("tm")
    s = lax.axis_index("space")
    even = lax.rem(t, 2) == 0
    odd = lax.rem(t, 2) == 1
    s_even = lax.rem(s, 2) == 0
    s_odd = lax.rem(s, 2) == 1
    partner = t + 1 - 2 * lax.rem(t, 2)
    ahead = lax.rem(t + 2, n_tm)
    behind = lax.rem(t + n_tm - 2, n_tm)
    next_up = lax.rem(t + 1, n_tm)
    prior = lax.rem(t + n_tm - 1, n_tm)
    has_lo = s > 0
    has_hi = s < n_space - 1
    inner = has_lo & has_hi
    rows = pl.ds(PAD, height)
    mine = pl.ds(1, planes)

    def lanes(c):
        return pl.ds(c * LANES, LANES)

    def scope(name):
        return jax.named_scope(name)

    load_g = [
        pltpu.make_async_copy(g_hbm.at[0, :, :, lanes(c)], V.at[0, c, mine, rows], load_sem.at[0])
        for c in range(chunks)
    ]
    loads = [
        pltpu.make_async_copy(k_hbm.at[0], K, load_sem.at[1]),
        pltpu.make_async_copy(m_hbm, M, load_sem.at[2]),
        pltpu.make_async_copy(f_hbm.at[0], F, load_sem.at[3]),
    ]

    barrier = pltpu.get_barrier_semaphore()
    first_z = t < 2
    last_z = t >= n_tm - 2
    near_z = (t >= n_tm - 4) & jnp.logical_not(last_z)
    by_token = t < n_tm - 4

    def greet(at, other):
        @pl.when(at)
        def _():
            pl.semaphore_signal(barrier, inc=1, device_id=other, device_id_type=MESH)

    def answer(at, token, other):
        @pl.when(at)
        def _():
            pl.semaphore_signal(token, inc=1, device_id=other, device_id_type=MESH)

    greet(first_z | last_z, {"tm": behind})
    greet(by_token, {"tm": ahead})
    greet(even, {"tm": partner})
    greet(s_odd, {"space": s - 1})
    greet(s_odd & has_hi, {"space": s + 1})

    @pl.when(jnp.logical_not(last_z))
    def _():
        for load in load_g + loads:
            load.start()

    one = jnp.int32(1)
    none = jnp.int32(0)
    told = jnp.where(first_z | last_z, none, one) + jnp.where(last_z | near_z, one, none) + jnp.where(odd, one, none)
    told = told + jnp.where(s_even & has_lo, one, none) + jnp.where(s_even & has_hi, one, none)
    with scope("bar"):
        for n in range(1, 6):
            @pl.when(told == n)
            def _(n=n):
                pl.semaphore_wait(barrier, n)
    answer(jnp.logical_not(first_z | last_z), token_z, {"tm": behind})
    answer(odd, token_x, {"tm": partner})
    answer(s_even & has_lo, token_s, {"space": s - 1})
    answer(s_even & has_hi, token_s, {"space": s + 1})

    def value(e, c):
        if e == 0:
            return g_hbm.at[0, :, :, lanes(c)]
        return V.at[2 * e, c, mine, rows]

    def plane(i, c, p):
        if i == 0:
            return g_hbm.at[0, p, :, lanes(c)]
        return V.at[i, c, 1 + p, rows]

    def alone(e, c, to_even):
        return WAY[e][c] == ("X" if to_even else "Z")

    def own_slot(e, c):
        return got.at[e, chunks + WAY[e][:c].count(WAY[e][c])]

    def z_got(e, c, to_even):
        return own_slot(e, c) if not to_even and alone(e, c, to_even) else got.at[e, c]

    def x_got(e, c, to_even):
        return own_slot(e, c) if to_even and alone(e, c, to_even) else got.at[e, c]

    def z_copy(e, c, src, to_even):
        return pltpu.make_async_remote_copy(
            src, ZB.at[e, c], zs, z_got(e, c, to_even), device_id={"tm": ahead}, device_id_type=MESH)

    def x_copy(e, c, src, to_even):
        return pltpu.make_async_remote_copy(
            src, XB.at[e, c], xs, x_got(e, c, to_even), device_id={"tm": partner}, device_id_type=MESH)

    def halo_sem(i, c):
        return h0 if i == 0 else hr.at[(i - 1) % 2, c]

    def to_lo(i, c):
        return pltpu.make_async_remote_copy(
            plane(i, c, 0), V.at[i, c, planes + 1, rows], hs, halo_sem(i, c),
            device_id={"space": s - 1}, device_id_type=MESH)

    def to_hi(i, c):
        return pltpu.make_async_remote_copy(
            plane(i, c, planes - 1), V.at[i, c, 0, rows], hs, halo_sem(i, c),
            device_id={"space": s + 1}, device_id_type=MESH)

    def send_halo(i, c):
        @pl.when(has_lo)
        def _():
            to_lo(i, c).start()

        @pl.when(has_hi)
        def _():
            to_hi(i, c).start()

    def landed(ref, sem):
        pltpu.make_async_remote_copy(
            ref, ref, hs, sem, device_id={"tm": partner}, device_id_type=MESH).wait_recv()

    def left(ref, sem):
        pltpu.make_async_remote_copy(
            ref, ref, sem, h0, device_id={"tm": partner}, device_id_type=MESH).wait_send()

    def wait_halo(i, c):
        which = pl.ds(0, chunks) if i == 0 else pl.ds(c, 1)
        for nb, at in ((2, inner), (1, jnp.logical_not(inner))):
            @pl.when(at)
            def _(nb=nb):
                landed(V.at[i, which, pl.ds(0, nb), rows], halo_sem(i, c))

    def first_halos():
        for c in range(chunks):
            send_halo(0, c)

    with scope("send0"):
        @pl.when(odd & jnp.logical_not(last_z))
        def _():
            for c in FIRST_X:
                x_copy(0, c, value(0, c), True).start()

        @pl.when(s_even & jnp.logical_not(last_z))
        def _():
            first_halos()

        @pl.when(by_token)
        def _():
            pl.semaphore_wait(token_z, 1)

        @pl.when(even)
        def _():
            for c in FIRST_EVEN:
                z_copy(0, c, value(0, c), True).start()

        @pl.when(odd)
        def _():
            for c in FIRST_ODD:
                z_copy(0, c, value(0, c), False).start()

        @pl.when(odd & last_z)
        def _():
            for c in FIRST_X:
                x_copy(0, c, value(0, c), True).start()

        @pl.when(last_z)
        def _():
            for load in load_g + loads:
                load.start()

        @pl.when(s_even & last_z)
        def _():
            first_halos()

    with scope("token_x"):
        @pl.when(even)
        def _():
            pl.semaphore_wait(token_x, 1)
            for c in range(chunks):
                x_copy(0, c, value(0, c), False).start()

    with scope("token_s"):
        @pl.when(s_odd & inner)
        def _():
            pl.semaphore_wait(token_s, 2)

        @pl.when(s_odd & jnp.logical_not(inner))
        def _():
            pl.semaphore_wait(token_s, 1)

        @pl.when(s_odd)
        def _():
            first_halos()

    edge = jnp.zeros((PAD, LANES), jnp.float32)
    flat = jnp.zeros((height, LANES), jnp.float32)

    def clear(c, _):
        for i in range(last + 1):
            for p in range(1, planes + 1):
                V[i, c, p, pl.ds(0, PAD), :] = edge
                V[i, c, p, pl.ds(PAD + height, PAD), :] = edge
        return 0

    def clear_plane(p):
        def body(c, _):
            for i in range(last + 1):
                V[i, c, p, rows, :] = flat
            return 0
        lax.fori_loop(0, chunks, body, 0)

    lax.fori_loop(0, chunks, clear, 0)

    @pl.when(jnp.logical_not(has_lo))
    def _():
        clear_plane(0)

    @pl.when(jnp.logical_not(has_hi))
    def _():
        clear_plane(planes + 1)

    with scope("loads"):
        pltpu.make_async_copy(V.at[0, :, mine, rows], V.at[0, :, mine, rows], load_sem.at[0]).wait()
        for load in loads:
            load.wait()

    def prepare(c, _):
        at = pl.ds(pl.multiple_of(c * LANES, LANES), LANES)
        for p in range(planes):
            k = K[p, :, at].astype(jnp.float32)
            m = M[p, :, at].astype(jnp.float32)
            d = 1.5 + 6.0 * k
            w = m / d
            W[c, p] = w
            FW[c, p] = w * F[p, :, at]
            KW[c, p] = k * w
            MD[c, p] = m * d
            MK[c, p] = m * k
        return 0

    lax.fori_loop(0, chunks, prepare, 0)

    lane = lax.broadcasted_iota(jnp.int32, (height, LANES), 1)

    def over_planes(body):
        def step(p, _):
            body(p)
            return 0
        lax.fori_loop(0, planes, step, 0, unroll=True)

    def beside(i, c, p, halo=True):
        mid = V[i, c, p + 1, rows, :]
        before = V[i, c - 1, p + 1, rows, :] if c > 0 else flat
        after = V[i, c + 1, p + 1, rows, :] if c < chunks - 1 else flat
        total = V[i, c, p + 1, pl.ds(PAD - 1, height), :]
        if halo or p > 0:
            total = total + V[i, c, p, rows, :]
        if halo or p < planes - 1:
            total = total + V[i, c, p + 2, rows, :]
        total = total + V[i, c, p + 1, pl.ds(PAD + 1, height), :]
        total = total + pltpu.roll(jnp.where(lane == LANES - 1, before, mid), 1, 1)
        total = total + pltpu.roll(jnp.where(lane == 0, after, mid), LANES - 1, 1)
        return mid, total

    def steps_before(e, c, p):
        z = ZB[e, c, p]
        both = 2.0 * XB[e, c, p] - 0.5 * z
        return jnp.where(even, z, both) if WAY[e][c] == "X" else both

    waited = set()

    def second(e, c):
        with scope(f"S{e}_{c}"):
            if WAY[e][c] == "X":
                @pl.when(even)
                def _():
                    landed(XB.at[e, c], x_got(e, c, True))

                    def mix(p):
                        CB[e, c, p] = 2.0 * XB[e, c, p] - 0.5 * V[2 * e, c, p + 1, rows, :]
                    over_planes(mix)
                    z_copy(e, c, CB.at[e, c], True).start()
            else:
                @pl.when(odd)
                def _():
                    if (e, c) not in waited:
                        landed(ZB.at[e, c], z_got(e, c, False))
                    x_copy(e, c, ZB.at[e, c], True).start()
                waited.add((e, c))

    def direct(e, c):
        with scope("direct"):
            @pl.when(odd)
            def _():
                if (e, c) == first_direct:
                    pl.semaphore_wait(token_d, 1)
                pltpu.make_async_remote_copy(
                    value(e, c), XB.at[e, c], xs, x_got(e, c, True),
                    device_id={"tm": next_up}, device_id_type=MESH).start()

    def ready(e, c):
        with scope(f"R{e}_{c}"):
            pair = XB.at[e, pl.ds(0, 2)]
            if WAY[e][c] == "D":
                landed(pair, got.at[e, c])
                return
            for to_even, at in ((True, even), (False, odd)):
                @pl.when(at)
                def _(to_even=to_even):
                    if not alone(e, c, to_even):
                        landed(pair, got.at[e, c])
                        return
                    landed(ZB.at[e, c] if to_even else XB.at[e, c], got.at[e, c])
                    if not to_even and (e, c) not in waited:
                        landed(ZB.at[e, c], z_got(e, c, False))
            waited.add((e, c))

    def sweep_first(e, c):
        with scope(f"H{e}_{c}"):
            if e > 0:
                wait_halo(2 * e, c)
            elif c == FIRST_SWEPT:
                wait_halo(0, 0)

        with scope(f"a{e}_{c}"):
            def early(p):
                mid, total = beside(2 * e, c, p)
                V[2 * e + 1, c, p + 1, rows, :] = FW[c, p] + KW[c, p] * total
            over_planes(early)
        ready(e, c)
        with scope(f"A{e}_{c}"):
            def step(p):
                g = W[c, p] * steps_before(e, c, p)
                G[c, p] = FW[c, p] + g
                V[2 * e + 1, c, p + 1, rows, :] = V[2 * e + 1, c, p + 1, rows, :] + g
            over_planes(step)
        send_halo(2 * e + 1, c)

    def sweep_second(e, c):
        n = e + 1
        i = 2 * e + 1

        def put(p, v):
            V[2 * n, c, p + 1, rows, :] = v
            if n == ITERS:
                p_out[0, p, :, lanes(c)] = v

        with scope(f"b{e}_{c}"):
            for p in range(planes):
                mid, total = beside(i, c, p, halo=False)
                v = G[c, p] + KW[c, p] * total
                if p in (0, planes - 1):
                    V[2 * n, c, p + 1, rows, :] = v
                else:
                    put(p, v)
        with scope(f"h{e}_{c}"):
            wait_halo(i, c)
        with scope(f"B{e}_{c}"):
            for p, beyond in ((0, 0), (planes - 1, planes + 1)):
                put(p, V[2 * n, c, p + 1, rows, :] + KW[c, p] * V[i, c, beyond, rows, :])

        @pl.when(even)
        def _():
            x_copy(n, c, value(n, c), False).start()
        send_halo(2 * n, c)

    def even_z(e, c):
        @pl.when(even)
        def _():
            z_copy(e, c, value(e, c), True).start()

    def odd_z(e, c):
        @pl.when(odd)
        def _():
            z_copy(e, c, value(e, c), False).start()

    def own_x(e, c):
        @pl.when(odd)
        def _():
            x_copy(e, c, value(e, c), True).start()

    def partial(e, c):
        with scope(f"Hl_{c}"):
            wait_halo(last, c)

        with scope(f"P_{c}"):
            def step(p):
                mid, total = beside(last, c, p)
                m = M[p, :, lanes(c)].astype(jnp.float32)
                G[c, p] = m * F[p, :, lanes(c)] - MD[c, p] * mid + MK[c, p] * total
            over_planes(step)

    def complete(e, c):
        ready(e, c)
        with scope(f"C_{c}"):
            def step(p):
                m = M[p, :, lanes(c)].astype(jnp.float32)
                r_out[0, p, :, lanes(c)] = G[c, p] + m * steps_before(ITERS, c, p)
            over_planes(step)

    acts = dict(S=second, A=sweep_first, B=sweep_second, E=even_z, O=odd_z, X=own_x, D=direct, P=partial, C=complete)
    relayed = next(c for name, e, c in STEPS if name == "A" and WAY[0][c] == "Z")
    first_direct = next(((e, c) for name, e, c in STEPS if name == "D"), None)
    for name, e, c in STEPS:
        acts[name](e, c)
        if first_direct and (name, e, c) == ("A", 0, relayed):
            answer(even, token_d, {"tm": prior})

    with scope("drain"):
        left(ZB, zs)
        left(XB, xs)
        for nb, at in ((2, inner), (1, jnp.logical_not(inner))):
            @pl.when(at)
            def _(nb=nb):
                left(V.at[:, :, pl.ds(0, nb), rows], hs)


def write_out(p_ref, r_ref, p_out, r_out, sem):
    copies = [
        pltpu.make_async_copy(src, dst, sem.at[i])
        for i, (src, dst) in enumerate(((p_ref, p_out), (r_ref, r_out)))
    ]
    for copy in copies:
        copy.start()
    for copy in copies:
        copy.wait()


def solution(mesh):
    n_tm, n_space = mesh.shape["tm"], mesh.shape["space"]
    placed = (
        P("tm", "space", None, None),
        P("tm", "space", None, None),
        P("space", None, None),
        P("tm", "space", None, None),
    )

    def body(forcing, inv_density, wall_mask, guess):
        planes, height, width = wall_mask.shape
        chunks = width // LANES
        full = (planes, height, width)
        cut = (chunks, planes, height, LANES)
        exchanges = ITERS + 1
        values = 2 * ITERS + 1
        f32 = jnp.float32
        pressure, residual = pl.pallas_call(
            functools.partial(kernel, n_tm, n_space),
            out_shape=[pltpu.VMEM(guess.shape, f32)] * 2,
            in_specs=[pl.BlockSpec(memory_space=pl.ANY)] * 4,
            out_specs=[pl.BlockSpec(memory_space=pltpu.VMEM)] * 2,
            scratch_shapes=[
                pltpu.VMEM((values, chunks, planes + 2, height + 2 * PAD, LANES), f32),
                pltpu.VMEM((exchanges,) + cut, f32),
                pltpu.VMEM((exchanges,) + cut, f32),
                pltpu.VMEM((exchanges,) + cut, f32),
                pltpu.VMEM(full, f32),
                pltpu.VMEM(full, inv_density.dtype),
                pltpu.VMEM(full, wall_mask.dtype),
                pltpu.VMEM(cut, f32),
                pltpu.VMEM(cut, f32),
                pltpu.VMEM(cut, f32),
                pltpu.VMEM(cut, f32),
                pltpu.VMEM(cut, f32),
                pltpu.VMEM(cut, f32),
                pltpu.SemaphoreType.DMA((4,)),
                pltpu.SemaphoreType.DMA,
                pltpu.SemaphoreType.DMA,
                pltpu.SemaphoreType.DMA((exchanges, chunks + chunks // 2)),
                pltpu.SemaphoreType.DMA,
                pltpu.SemaphoreType.DMA((2, chunks)),
                pltpu.SemaphoreType.DMA,
                pltpu.SemaphoreType.REGULAR,
                pltpu.SemaphoreType.REGULAR,
                pltpu.SemaphoreType.REGULAR,
                pltpu.SemaphoreType.REGULAR,
            ],
            compiler_params=pltpu.CompilerParams(collective_id=0, has_side_effects=True),
        )(forcing, inv_density, wall_mask, guess)
        return pl.pallas_call(
            write_out,
            out_shape=(jax.ShapeDtypeStruct(guess.shape, f32),) * 2,
            in_specs=[pl.BlockSpec(memory_space=pltpu.VMEM)] * 2,
            out_specs=(pl.BlockSpec(memory_space=pl.ANY),) * 2,
            scratch_shapes=[pltpu.SemaphoreType.DMA((2,))],
        )(*[pltpu.with_memory_space_constraint(v, pltpu.VMEM) for v in (pressure, residual)])

    return jax.shard_map(
        body,
        mesh=mesh,
        in_specs=placed,
        out_specs=(P("tm", "space", None, None), P("tm", "space", None, None)),
        check_vma=False,
    )
```
